128 devices in a mesh: row: 64 (over z, y, x), col: 2 (over core).
Axes of the slice: x: 4, y: 4, z: 4, core: 2. Of those that a mesh axis runs over, the one named last changes fastest.
Arguments:
- vectors_in: bfloat16 [131072, 2048], P('row', 'col'), may hold values from -6 to 6
- panel: bfloat16 [131072, 256], P('row', 'col'), may hold values from -0.015625 to 0.015625
- factor: float32 [256, 256], replicated, may hold values from -3 to 8, as said below
- atom_basis: int32 [64, 128], P('row'), may hold values from 1 to 24, 2048 in all within a row
- proj_count: int32 [8192], P('row'), may hold values from 1 to 16
- coupling: bfloat16 [8192, 9, 384], P('row'), may hold values from -0.4375 to 0.4375
- block_present: int32 [8192, 9], P('row'), may hold values 0 or 1
- occ_mask: int32 [2048], P('col'), may hold values 0 or 1
- occ_weight: float32 [2048], P('col'), may hold values from 0.5 to 2
Outputs:
- vectors: bfloat16 [131072, 2048], P('row', 'col')
- density: float32 [8192, 256], P(('row', 'col'))
The draws below stay inside these ranges and needn't reach their ends.
Inputs may be any that keep to these rules, and one draw needn't show every extreme that they name: `factor`: zero below the diagonal; the diagonal lies in 4 to 8. `atom_basis`: each row sums to 2048, and 24 is reached in each row.
All inputs are finite; a program needn't handle non-finite values. No bound on the sum of `block_present` or of `occ_mask` on one device may be relied on, other than what follows from the above.
Results may differ from the reference program's by a relative error of at most 0.0075.
Values may be sent and summed in bfloat16 or wider, within the bound.
No kernel may reach another device: no remote copies, remote signals or barrier semaphores. Data moves between devices by JAX's collectives and lax.ppermute only.
A program may use at most 192 MiB of HBM per device.

```python
import math
import jax
import jax.numpy as jnp
import numpy as np
from jax import lax

M_DEV = 2048
NB_DEV = 1024
NPAN = 256
NPMAX = 16
BMAX = 24
K = 9
A_DEV = 128
M = 131072
NB = 2048
ATOMS = 8192
N_ROW = 64
N_COL = 2


def draw_factor(key, part):
    key_upper, key_diagonal = jax.random.split(key, 2)
    upper = jnp.clip(jax.random.normal(key_upper, (NPAN, NPAN), jnp.float32), -6.0, 6.0) * 0.5
    diagonal = jax.random.uniform(key_diagonal, (NPAN,), jnp.float32, 4.0, 8.0)
    return jnp.triu(upper, 1) + jnp.diag(diagonal)


def place_ends(values, rng, least, high):
    longest = values.shape.index(max(values.shape))
    spots = []
    for shift in (0, 1):
        where = [jax.random.randint(jax.random.fold_in(rng, axis), (), 0, length) for axis, length in enumerate(values.shape)]
        where[longest] = (where[longest] + shift) % values.shape[longest]
        spots.append(tuple(where))
    return values.at[spots[0]].set(least).at[spots[1]].set(high)


def steps_of(key, dims, cuts, smallest, high):
    level, own = 1.0, jax.random.fold_in(key, 6)
    for axis_at, parts in cuts:
        draws = jnp.exp(jax.random.uniform(jax.random.fold_in(own, axis_at), (parts,), jnp.float32, smallest / len(cuts), high / len(cuts)))
        level = level * jnp.repeat(draws, dims[axis_at] // parts).reshape([-1 if axis == axis_at else 1 for axis in range(len(dims))])
    return level


def split_up(number_of, total, most, skew):
    weights = [(1 << 20) // math.isqrt(rank ** skew) + 1 for rank in range(2, number_of + 1)]
    spare, holding = total - most - (number_of - 1), [1] * (number_of - 1)
    while spare > 0:
        candidates = [i for i in range(number_of - 1) if holding[i] < most]
        mass, left = sum([weights[i] for i in candidates]), spare
        for i in candidates:
            extra = min(most - holding[i], max(1, left * weights[i] // mass), spare)
            holding[i] = holding[i] + extra
            spare = spare - extra
    return np.array([most] + holding)


def ragged(rng, amount, total, limit, skew):
    if amount == 2:
        one = jax.random.randint(rng, (), max(1, total - limit), min(limit, total - 1) + 1)
        return jnp.stack([one, total - one])
    tallies = jnp.asarray(split_up(amount, total, limit, skew), jnp.int32)
    pairs = (amount - 1) // 2
    source_of, receiver = tallies[1:1 + 2 * pairs:2], tallies[2:2 + 2 * pairs:2]
    slack = jnp.minimum(source_of - 1, limit - receiver)
    moved = jax.random.randint(jax.random.fold_in(rng, 1), (pairs,), 0, 1 << 20) % (slack + 1)
    tallies = tallies.at[1:1 + 2 * pairs:2].set(source_of - moved).at[2:2 + 2 * pairs:2].set(receiver + moved)
    return tallies[jax.random.permutation(jax.random.fold_in(rng, 2), amount)]


def bell_draw(rng, extent, width, reach, cuts=(), held_as=jnp.bfloat16):
    array = jax.random.normal(rng, extent, jnp.float32) * width
    if len(cuts) > 0:
        array = steps_of(rng, extent, cuts, -0.22, 0.18) * array
    return jnp.clip(array, min=-reach, max=reach).astype(held_as)


def setup_inputs(seed: int = 0) -> dict:
    splits = jax.random.split(jax.random.key(seed), 10)
    return {
        "vectors_in": bell_draw(splits[0], (M, NB), 1.0, 6.0, ((0, 64), (1, 2))),
        "panel": bell_draw(splits[1], (M, NPAN), M ** -0.5, 0.015625, ((0, 64), (1, 2))),
        "factor": draw_factor(jax.random.fold_in(splits[9], 71), 0),
        "atom_basis": jax.vmap(lambda own: ragged(own, A_DEV, M_DEV, BMAX, 0))(jax.random.split(splits[3], N_ROW)).reshape((N_ROW, A_DEV)).astype(jnp.int32),
        "proj_count": place_ends(jax.random.randint(splits[4], (ATOMS,), 1, NPMAX + 1), jax.random.fold_in(splits[4], 1), 1, NPMAX).astype(jnp.int32),
        "coupling": bell_draw(splits[5], (ATOMS, K, NPMAX * BMAX), (K * BMAX) ** -0.5, 0.4375, ((0, 64),)),
        "block_present": place_ends((jax.random.randint(splits[6], (ATOMS, K), 0, 4) < 3).astype(jnp.int32), jax.random.fold_in(splits[6], 1), 0, 1),
        "occ_mask": place_ends((jax.random.randint(splits[7], (NB,), 0, 4) < 3).astype(jnp.int32), jax.random.fold_in(splits[7], 1), 0, 1),
        "occ_weight": jnp.clip(jnp.exp(math.log(2.0) - 1.3862944 * jax.random.uniform(splits[8], (NB,), jnp.float32) ** steps_of(splits[8], (NB,), ((0, 2),), -0.2, 0.2)), 0.5, 2.0),
    }


def reference(vectors_in, panel, factor, atom_basis, proj_count, coupling, block_present, occ_mask, occ_weight):
    column_blocks = vectors_in.reshape(N_ROW, M_DEV, NB)
    panel_blocks = panel.reshape(N_ROW, M_DEV, NPAN)

    def accumulate(running, pair):
        product = lax.dot_general(pair[1], pair[0], (((0,), (0,)), ((), ())), preferred_element_type=jnp.float32)
        return running + product, None

    inner_products, leftover = lax.scan(accumulate, jnp.zeros((NPAN, NB), jnp.float32), (column_blocks, panel_blocks))
    mixing = jnp.dot(factor.T, inner_products, precision=lax.Precision.HIGHEST).astype(jnp.bfloat16)

    def rotate(pair):
        update = jnp.dot(pair[1], mixing, preferred_element_type=jnp.float32)
        return (pair[0].astype(jnp.float32) - update).astype(jnp.bfloat16)

    vectors = lax.map(rotate, (column_blocks, panel_blocks)).reshape(N_ROW * M_DEV, NB)

    counts = atom_basis.astype(jnp.int32)
    starts = jnp.cumsum(counts, axis=1).astype(jnp.int32) - counts
    starts = starts + jnp.arange(N_ROW, dtype=jnp.int32)[:, None] * M_DEV
    starts = starts.reshape(-1)
    counts_flat = counts.reshape(-1)
    slot_rank = jnp.arange(BMAX, dtype=jnp.int32)
    row_index = jnp.where(slot_rank[None, :] < counts_flat[:, None], starts[:, None] + slot_rank[None, :], N_ROW * M_DEV).astype(jnp.int32).reshape(-1)
    kept_rows = (jnp.arange(NPMAX, dtype=jnp.int32)[None, :] < proj_count[:, None]).astype(jnp.float32)
    weights = occ_mask.astype(jnp.float32) * occ_weight / NB
    rim_width = (K - 1) // 2

    def column_block(running, block_number):
        columns = lax.dynamic_slice_in_dim(vectors, block_number * NB_DEV, NB_DEV, 1)
        padded = jnp.take(columns, row_index, axis=0, mode="fill", fill_value=0).reshape(ATOMS, BMAX, NB_DEV).astype(jnp.float32)
        projections = jnp.zeros((ATOMS, NPMAX, NB_DEV), jnp.float32)
        for relative in range(K):
            blocks = coupling[:, relative].reshape(ATOMS, NPMAX, BMAX)
            blocks = jnp.where(block_present[:, relative, None, None] > 0, blocks, jnp.zeros_like(blocks)).astype(jnp.float32)
            neighbours = jnp.roll(padded, rim_width - relative, axis=0)
            projections = projections + jnp.einsum("aij,ajn->ain", blocks, neighbours, precision=lax.Precision.HIGHEST)
        rounded = (projections * kept_rows[:, :, None]).astype(jnp.bfloat16)
        local_weights = lax.dynamic_slice_in_dim(weights, block_number * NB_DEV, NB_DEV, 0)
        weighted = (rounded.astype(jnp.float32) * local_weights[None, None, :]).astype(jnp.bfloat16)
        partial_value = jnp.einsum("ain,ajn->aij", weighted.astype(jnp.float32), rounded.astype(jnp.float32), precision=lax.Precision.HIGHEST)
        return running + partial_value.reshape(ATOMS, NPMAX * NPMAX), None

    density, remains = lax.scan(column_block, jnp.zeros((ATOMS, NPMAX * NPMAX), jnp.float32), jnp.arange(N_COL, dtype=jnp.int32))
    return vectors, density
```

```python
import functools

import jax
import jax.numpy as jnp
from jax import lax
from jax.experimental import pallas as pl
from jax.experimental.pallas import tpu as pltpu
from jax.sharding import PartitionSpec as P

NPMAX = 16
BMAX = 24
K = 9
RIM = 4
EDGE = RIM * BMAX
GROUP = 16
SPAN = GROUP + 2 * RIM
WIDE = 640
ALIGN = 64
MIB = 1024 * 1024

VM = pltpu.MemorySpace.VMEM
SM = pltpu.MemorySpace.SMEM
NT = (((1,), (1,)), ((), ()))
NN = (((1,), (0,)), ((), ()))


def dot(a, b, dims=NN, **kw):
    return lax.dot_general(a, b, dims, preferred_element_type=jnp.float32, **kw)


def iota(shape, dim):
    return lax.broadcasted_iota(jnp.int32, shape, dim)


def padded_rows(counts_ref, first_atom, first_row, base_row, sources):
    depth = sources[0].shape[0]
    slot = iota((EDGE, 1), 0)
    target = jnp.full((EDGE, 1), -1, jnp.int32)
    row = first_row - base_row
    for t in range(RIM):
        count = counts_ref[first_atom + t]
        u = slot - t * BMAX
        target = jnp.where((u >= 0) & (u < count), row + u, target)
        row = row + count
    pick = (iota((EDGE, depth), 1) == target).astype(jnp.float32).astype(jnp.bfloat16)
    return [dot(pick, s).astype(jnp.bfloat16) for s in sources]


def halo_kernel(counts_ref, v_top, v_end, own_top, own_end, other_top, other_end, to_next, to_last):
    atoms = counts_ref.shape[0]
    rows = EDGE + 32
    tail = counts_ref[atoms - 1]
    for t in range(1, RIM):
        tail = tail + counts_ref[atoms - 1 - t]
    cols = v_top.shape[1]
    half = own_top.shape[1]
    last = padded_rows(
        counts_ref, atoms - RIM, rows - tail, 0, [v_end[...], own_end[...], other_end[...]]
    )
    first = padded_rows(counts_ref, 0, 0, 0, [v_top[...], own_top[...], other_top[...]])
    for out, pieces in ((to_next, last), (to_last, first)):
        out[:, :cols] = pieces[0]
        out[:, cols : cols + half] = pieces[1]
        out[:, cols + half :] = pieces[2]


def band_kernel(counts_ref, cm_ref, band_ref, start_ref, pos_ref, cp_ref):
    atoms = counts_ref.shape[0]
    groups = atoms // GROUP
    rows = groups * 256
    for t in range(RIM):
        pos_ref[t] = t * BMAX
        pos_ref[RIM + atoms + t] = EDGE + rows + t * BMAX

    def add(t, at):
        pos_ref[RIM + t] = at
        return at + counts_ref[t]

    lax.fori_loop(0, atoms, add, jnp.int32(EDGE))
    lane = iota((8, WIDE), 1)
    which = lane // BMAX
    slot = lane - which * BMAX
    sub = iota((GROUP, NPMAX * BMAX), 1) // BMAX
    for g in range(groups):
        first = pos_ref[g * GROUP]
        start = jnp.minimum((first // ALIGN) * ALIGN, rows + 2 * EDGE - WIDE)
        start_ref[g] = start
        target = jnp.full((8, WIDE), -1, jnp.int32)
        for t in range(SPAN):
            atom = g * GROUP + t - RIM
            count = counts_ref[atom] if 0 <= atom < atoms else BMAX
            at = pos_ref[atom + RIM] - start
            target = jnp.where((which == t) & (slot < count), at + slot, target)
        pick = (iota((WIDE, WIDE), 0) == target[:1]).astype(jnp.float32).astype(jnp.bfloat16)
        x = [cm_ref[k, g * GROUP : (g + 1) * GROUP, :].astype(jnp.float32) for k in range(K)]
        x += [None] * (NPMAX - K)
        lanes = NPMAX * BMAX
        for bit in (1, 2, 4, 8):
            low = (sub // bit) % 2 == 0
            new = list(x)
            for p in range(NPMAX):
                q = p + bit
                if p & bit or (x[p] is None and x[q] is None):
                    continue
                a, b = x[p], x[q]
                zero = jnp.zeros((GROUP, lanes), jnp.float32)
                b_up = zero if b is None else pltpu.roll(b, bit * BMAX, 1)
                a_down = zero if a is None else pltpu.roll(a, lanes - bit * BMAX, 1)
                new[p] = jnp.where(low, zero if a is None else a, b_up)
                new[q] = jnp.where(low, a_down, zero if b is None else b)
            x = new
        pad = jnp.zeros((GROUP, WIDE - lanes), jnp.float32)
        for i in range(NPMAX):
            wide = jnp.concatenate([x[i], pad], axis=1)
            halves = [wide[:8], pltpu.roll(wide[8:], 8 * BMAX, 1)]
            for _ in range(2):
                halves = [pltpu.roll(h, 0, 1, stride=BMAX // 2, stride_axis=0) for h in halves]
            skew = jnp.concatenate(halves, axis=0)
            cp_ref[i * GROUP : (i + 1) * GROUP, :] = skew.astype(jnp.bfloat16)
        band_ref[g] = dot(cp_ref[...], pick, NT).astype(jnp.bfloat16)


def inner_kernel(own_ref, other_ref, v_ref, out_ref, pt_ref):
    half = own_ref.shape[1]

    @pl.when(pl.program_id(0) == 0)
    def _():
        pt_ref[:half, :] = own_ref[...].T
        pt_ref[half:, :] = other_ref[...].T

    out_ref[...] = dot(pt_ref[...], v_ref[...]).T


def mix_kernel(parts_ref, factor_ref, out_ref):
    total = jnp.sum(parts_ref[...], axis=0)
    mixed = dot(total, factor_ref[...], precision=lax.Precision.HIGHEST).astype(jnp.bfloat16)
    out_ref[...] = jnp.broadcast_to(mixed[None], out_ref.shape)


def main_kernel(
    col_ref,
    start_ref,
    mix_ref,
    before_ref,
    after_ref,
    weight_ref,
    own_ref,
    other_ref,
    v_hbm,
    band_hbm,
    vectors_hbm,
    own_out,
    other_out,
    v_ref,
    band_ref,
    e_ref,
    v_sem,
    band_sem,
    out_sem,
):
    rows, cols = v_hbm.shape
    blocks = rows // 256
    groups = band_ref.shape[0]
    v_copies, out_copies = [], []
    for b in range(blocks):
        at = pl.ds(b * 256, 256)
        v_copies.append(pltpu.make_async_copy(v_hbm.at[at], v_ref.at[at], v_sem.at[b]))
        out_copies.append(
            pltpu.make_async_copy(
                e_ref.at[pl.ds(EDGE + b * 256, 256)], vectors_hbm.at[at], out_sem.at[b]
            )
        )
        v_copies[-1].start()
    band_copy = pltpu.make_async_copy(band_hbm, band_ref, band_sem)
    band_copy.start()
    mix = mix_ref[...]

    def rotated(vectors, panel):
        return (vectors.astype(jnp.float32) - dot(panel, mix, NT)).astype(jnp.bfloat16)

    e_ref[:EDGE, :] = rotated(before_ref[:, :cols], before_ref[:, cols:])
    e_ref[EDGE + rows :, :] = rotated(after_ref[:, :cols], after_ref[:, cols:])
    for b in range(blocks):
        v_copies[b].wait()
        at = slice(b * 256, (b + 1) * 256)
        panel = jnp.concatenate([own_ref[at, :], other_ref[at, :]], axis=1)
        e_ref[EDGE + b * 256 : EDGE + (b + 1) * 256, :] = rotated(v_ref[at, :], panel)
        out_copies[b].start()
    band_copy.wait()
    weight = weight_ref[...]
    down, along = iota((256, 256), 0), iota((256, 256), 1)
    same_atom = (down % GROUP) == (along % GROUP)
    spread = ((down // GROUP) == (along % NPMAX)).astype(jnp.float32).astype(jnp.bfloat16)
    same_i = (down // GROUP) == (along // NPMAX)
    per = groups // 2
    col = col_ref[0]
    for turn in range(2):
        out = other_out if turn == 0 else own_out
        side = (1 - col) if turn == 0 else col
        for step in range(per):
            g = side * per + step
            window = e_ref[pl.ds(pl.multiple_of(start_ref[g], ALIGN), WIDE), :]
            rounded = dot(band_ref[g], window).astype(jnp.bfloat16)
            weighted = (rounded.astype(jnp.float32) * weight).astype(jnp.bfloat16)
            pairs = jnp.where(same_atom, dot(weighted, rounded, NT), 0.0)
            high = pairs.astype(jnp.bfloat16)
            low = (pairs - high.astype(jnp.float32)).astype(jnp.bfloat16)
            spreaded = jnp.where(same_i, dot(high, spread) + dot(low, spread), 0.0)
            total = spreaded[:GROUP]
            for i in range(1, NPMAX):
                total = total + spreaded[i * GROUP : (i + 1) * GROUP]
            out[step * GROUP : (step + 1) * GROUP, :] = total
    for c in out_copies:
        c.wait()


def call(kernel, out_shape, in_specs, out_specs, flops, nbytes, mib, **kw):
    return pl.pallas_call(
        kernel,
        out_shape=out_shape,
        in_specs=in_specs,
        out_specs=out_specs,
        compiler_params=pltpu.CompilerParams(vmem_limit_bytes=mib * MIB),
        cost_estimate=pl.CostEstimate(flops=flops, bytes_accessed=nbytes, transcendentals=0),
        **kw,
    )


def local(
    vectors_in, panel, factor, atom_basis, proj_count, coupling, block_present, occ_mask, occ_weight
):
    rows, cols = vectors_in.shape
    half = panel.shape[1]
    npan = 2 * half
    counts = atom_basis[0]
    atoms = counts.shape[0]
    groups = atoms // GROUP
    n_row = lax.axis_size("row")
    n_col = lax.axis_size("col")
    col = lax.axis_index("col")
    vmem = pl.BlockSpec(memory_space=VM)
    smem = pl.BlockSpec(memory_space=SM)
    hbm = pl.BlockSpec(memory_space=pltpu.MemorySpace.HBM)
    bf16, f32 = jnp.bfloat16, jnp.float32

    other = lax.ppermute(panel, "col", [(0, 1), (1, 0)])

    tile = 256
    partial = pl.pallas_call(
        inner_kernel,
        out_shape=jax.ShapeDtypeStruct((cols, npan), f32),
        grid=(cols // tile,),
        in_specs=[
            pl.BlockSpec((rows, half), lambda c: (0, 0)),
            pl.BlockSpec((rows, half), lambda c: (0, 0)),
            pl.BlockSpec((rows, tile), lambda c: (0, c)),
        ],
        out_specs=pl.BlockSpec((tile, npan), lambda c: (c, 0)),
        scratch_shapes=[pltpu.VMEM((npan, rows), bf16)],
        compiler_params=pltpu.CompilerParams(vmem_limit_bytes=16 * MIB),
        cost_estimate=pl.CostEstimate(
            flops=2 * rows * cols * npan, bytes_accessed=6 << 20, transcendentals=0
        ),
    )(panel, other, vectors_in)
    slices = lax.all_to_all(partial, "row", 0, 0, tiled=True)
    slices = slices.reshape(n_row, cols // n_row, npan)
    flipped = jnp.roll(jnp.roll(factor, half, axis=0), half, axis=1)
    ordered = jnp.where(col == 0, factor, flipped)
    copies = call(
        mix_kernel,
        jax.ShapeDtypeStruct((n_row, cols // n_row, npan), bf16),
        [vmem, vmem],
        vmem,
        1 << 24,
        2 << 20,
        8,
    )(slices, ordered)
    mixing = lax.all_to_all(copies.reshape(cols, npan), "row", 0, 0, tiled=True)

    edge = EDGE + 32
    to_next, to_last = call(
        halo_kernel,
        [jax.ShapeDtypeStruct((EDGE, cols + npan), bf16)] * 2,
        [smem] + [vmem] * 6,
        [vmem, vmem],
        1 << 26,
        2 << 20,
        8,
    )(
        counts,
        vectors_in[:edge],
        vectors_in[rows - edge :],
        panel[:edge],
        panel[rows - edge :],
        other[:edge],
        other[rows - edge :],
    )
    up = [(i, (i + 1) % n_row) for i in range(n_row)]
    before = lax.ppermute(to_next, "row", up)
    after = lax.ppermute(to_last, "row", [(j, i) for i, j in up])

    which = jnp.arange(NPMAX * BMAX, dtype=jnp.int32) // BMAX
    keep = (block_present.T[:, :, None] > 0) & (which[None, None, :] < proj_count[None, :, None])
    blocks = coupling.transpose(1, 0, 2)
    blocks = jnp.where(keep, blocks, jnp.zeros_like(blocks))
    band, starts = call(
        band_kernel,
        [
            jax.ShapeDtypeStruct((groups, 256, WIDE), bf16),
            jax.ShapeDtypeStruct((groups,), jnp.int32),
        ],
        [smem, vmem],
        [vmem, smem],
        groups * 2 * 256 * WIDE * WIDE,
        4 << 20,
        16,
        scratch_shapes=[pltpu.SMEM((atoms + 2 * RIM,), jnp.int32), pltpu.VMEM((256, WIDE), bf16)],
    )(counts, blocks)

    weights = (occ_mask.astype(f32) * occ_weight / (cols * n_col))[None, :]
    vectors, own_part, other_part = call(
        main_kernel,
        [
            jax.ShapeDtypeStruct((rows, cols), bf16),
            jax.ShapeDtypeStruct((atoms // 2, 256), f32),
            jax.ShapeDtypeStruct((atoms // 2, 256), f32),
        ],
        [smem, smem] + [vmem] * 6 + [hbm] * 2,
        [hbm, vmem, vmem],
        10 << 30,
        14 << 20,
        50,
        scratch_shapes=[
            pltpu.VMEM((rows, cols), bf16),
            pltpu.VMEM((groups, 256, WIDE), bf16),
            pltpu.VMEM((rows + 2 * EDGE, cols), bf16),
            pltpu.SemaphoreType.DMA((rows // 256,)),
            pltpu.SemaphoreType.DMA,
            pltpu.SemaphoreType.DMA((rows // 256,)),
        ],
    )(col[None], starts, mixing, before, after, weights, panel, other, vectors_in, band)
    density = own_part + lax.ppermute(other_part, "col", [(0, 1), (1, 0)])
    return vectors, density


def solution(mesh):
    placed = (
        P("row", "col"),
        P("row", "col"),
        P(),
        P("row", None),
        P("row"),
        P("row", None, None),
        P("row", None),
        P("col"),
        P("col"),
    )
    return jax.shard_map(
        local,
        mesh=mesh,
        in_specs=placed,
        out_specs=(P("row", "col"), P(("row", "col"), None)),
        check_vma=False,
    )
```

```python
import functools

import jax
import jax.numpy as jnp
from jax import lax
from jax.experimental import pallas as pl
from jax.experimental.pallas import tpu as pltpu
from jax.sharding import PartitionSpec as P

NPMAX = 16
BMAX = 24
K = 9
RIM = 4
EDGE = RIM * BMAX
TAIL = 128
GROUP = 16
SPAN = GROUP + 2 * RIM
WIDE = 640
ALIGN = 64
MIB = 1024 * 1024

VM = pltpu.MemorySpace.VMEM
SM = pltpu.MemorySpace.SMEM
NT = (((1,), (1,)), ((), ()))
NN = (((1,), (0,)), ((), ()))


def dot(a, b, dims=NN, **kw):
    return lax.dot_general(a, b, dims, preferred_element_type=jnp.float32, **kw)


def iota(shape, dim):
    return lax.broadcasted_iota(jnp.int32, shape, dim)


def padded_rows(counts_ref, first_atom, first_row, source):
    slot = iota((EDGE, 1), 0)
    target = jnp.full((EDGE, 1), -1, jnp.int32)
    row = first_row
    for t in range(RIM):
        count = counts_ref[first_atom + t]
        u = slot - t * BMAX
        target = jnp.where((u >= 0) & (u < count), row + u, target)
        row = row + count
    pick = (iota((EDGE, TAIL), 1) == target).astype(jnp.float32).astype(jnp.bfloat16)
    return dot(pick, source).astype(jnp.bfloat16)


def halo_kernel(
    counts_ref, v_hbm, own_hbm, other_hbm, partial_hbm, to_next, to_last, rows_ref, sem
):
    atoms = counts_ref.shape[0]
    rows, cols = v_hbm.shape
    half = own_hbm.shape[1]
    spans = ((0, cols), (cols, half), (cols + half, half))
    copies = []
    for n, first in enumerate((0, rows - TAIL)):
        for m, (src, (at, width)) in enumerate(zip((v_hbm, own_hbm, other_hbm), spans)):
            copies.append(
                pltpu.make_async_copy(
                    src.at[pl.ds(first, TAIL)],
                    rows_ref.at[n, :, pl.ds(at, width)],
                    sem.at[n, m],
                )
            )
            copies[-1].start()
    tail = counts_ref[atoms - 1]
    for t in range(1, RIM):
        tail = tail + counts_ref[atoms - 1 - t]
    for c in copies:
        c.wait()
    to_next[...] = padded_rows(counts_ref, atoms - RIM, TAIL - tail, rows_ref[1])
    to_last[...] = padded_rows(counts_ref, 0, 0, rows_ref[0])


def pre_kernel(
    first_group,
    counts_ref,
    present_ref,
    proj_ref,
    cm_ref,
    halo_ref,
    v_hbm,
    own_hbm,
    other_hbm,
    u_hbm,
    t_hbm,
    mark_ref,
    pos_ref,
    cp_ref,
    mask_ref,
    column_ref,
    e_ref,
    p_ref,
    u_ref,
    t_ref,
    sem,
    out_sem,
):
    atoms = counts_ref.shape[0]
    rows, cols = v_hbm.shape
    half = own_hbm.shape[1]
    inner = pl.ds(EDGE, rows)
    copies = [
        pltpu.make_async_copy(v_hbm, e_ref.at[inner], sem.at[0]),
        pltpu.make_async_copy(own_hbm, p_ref.at[inner, pl.ds(0, half)], sem.at[1]),
        pltpu.make_async_copy(other_hbm, p_ref.at[inner, pl.ds(half, half)], sem.at[2]),
    ]
    for c in copies:
        c.start()
    out_copies = []
    mine, unread = (0, EDGE + rows) if first_group == 0 else (EDGE + rows, 0)
    e_ref[mine : mine + EDGE, :] = halo_ref[:, :cols]
    p_ref[mine : mine + EDGE, :] = halo_ref[:, cols:]
    e_ref[unread : unread + EDGE, :] = jnp.zeros((EDGE, cols), jnp.bfloat16)
    p_ref[unread : unread + EDGE, :] = jnp.zeros((EDGE, 2 * half), jnp.bfloat16)
    mark_ref[0] = counts_ref[0]

    for t in range(RIM):
        pos_ref[t] = t * BMAX
        pos_ref[RIM + atoms + t] = EDGE + rows + t * BMAX

    def add(t, at):
        pos_ref[RIM + t] = at
        return at + counts_ref[t]

    lax.fori_loop(0, atoms, add, jnp.int32(EDGE), unroll=8)
    mask_ref[...] = jnp.zeros(mask_ref.shape, jnp.float32)
    mask_ref[:K, :] = present_ref[...].astype(jnp.float32)
    mask_ref[K : K + 1, :] = proj_ref[...].astype(jnp.float32)
    column_ref[...] = mask_ref[...].T
    lanes = NPMAX * BMAX
    lane = iota((8, WIDE), 1)
    which = lane // BMAX
    slot = lane - which * BMAX
    sub = iota((GROUP, lanes), 1) // BMAX
    for n in range(u_ref.shape[0]):
        g = first_group + n
        mine = slice(g * GROUP, (g + 1) * GROUP)
        first = pos_ref[g * GROUP]
        start = jnp.minimum((first // ALIGN) * ALIGN, rows + 2 * EDGE - WIDE)
        target = jnp.full((8, WIDE), -1, jnp.int32)
        for t in range(SPAN):
            atom = g * GROUP + t - RIM
            count = counts_ref[atom] if 0 <= atom < atoms else BMAX
            at = pos_ref[atom + RIM] - start
            target = jnp.where((which == t) & (slot < count), at + slot, target)
        pick = (iota((WIDE, WIDE), 0) == target[:1]).astype(jnp.float32).astype(jnp.bfloat16)
        kept = column_ref[mine, K : K + 1] > sub.astype(jnp.float32)
        x = []
        for k in range(K):
            block = cm_ref[k, mine, :].astype(jnp.float32)
            x.append(jnp.where((column_ref[mine, k : k + 1] > 0.0) & kept, block, 0.0))
        x += [None] * (NPMAX - K)
        for bit in (1, 2, 4, 8):
            low = (sub // bit) % 2 == 0
            new = list(x)
            for p in range(NPMAX):
                q = p + bit
                if p & bit or (x[p] is None and x[q] is None):
                    continue
                a, b = x[p], x[q]
                zero = jnp.zeros((GROUP, lanes), jnp.float32)
                b_up = zero if b is None else pltpu.roll(b, bit * BMAX, 1)
                a_down = zero if a is None else pltpu.roll(a, lanes - bit * BMAX, 1)
                new[p] = jnp.where(low, zero if a is None else a, b_up)
                new[q] = jnp.where(low, a_down, zero if b is None else b)
            x = new
        pad = jnp.zeros((GROUP, WIDE - lanes), jnp.float32)
        for i in range(NPMAX):
            wide = jnp.concatenate([x[i], pad], axis=1)
            halves = [wide[:8], pltpu.roll(wide[8:], 8 * BMAX, 1)]
            for _ in range(2):
                halves = [pltpu.roll(h, 0, 1, stride=BMAX // 2, stride_axis=0) for h in halves]
            skew = jnp.concatenate(halves, axis=0)
            cp_ref[n, i * GROUP : (i + 1) * GROUP, :] = skew.astype(jnp.bfloat16)
        band = dot(cp_ref[n], pick, NT).astype(jnp.bfloat16)
        if n == 0:
            for c in copies:
                c.wait()
        window = pl.ds(pl.multiple_of(start, ALIGN), WIDE)
        u_ref[n] = dot(band, e_ref[window, :]).astype(jnp.bfloat16)
        t_ref[n] = dot(band, p_ref[window, :]).astype(jnp.bfloat16)
        out_copies.append(pltpu.make_async_copy(u_ref.at[n], u_hbm.at[n], out_sem.at[0, n]))
        out_copies.append(pltpu.make_async_copy(t_ref.at[n], t_hbm.at[n], out_sem.at[1, n]))
        for c in out_copies[-2:]:
            c.start()
    for c in out_copies:
        c.wait()


def inner_kernel(own_ref, other_ref, v_ref, out_ref, pt_ref):
    half = own_ref.shape[1]

    @pl.when(pl.program_id(0) == 0)
    def _():
        pt_ref[:half, :] = own_ref[...].T
        pt_ref[half:, :] = other_ref[...].T

    out_ref[...] = dot(pt_ref[...], v_ref[...]).T.astype(jnp.bfloat16)


def mix_kernel(mark_ref, parts_ref, factor_ref, out_ref):
    total = jnp.sum(parts_ref[...].astype(jnp.float32), axis=0)
    mixed = dot(total, factor_ref[...], precision=lax.Precision.HIGHEST).astype(jnp.bfloat16)
    out_ref[...] = jnp.broadcast_to(mixed[None], out_ref.shape)


def main_kernel(
    col_ref,
    mix_ref,
    weight_ref,
    own_ref,
    other_ref,
    u_low,
    t_low,
    u_high,
    t_high,
    v_hbm,
    vectors_hbm,
    own_out,
    other_out,
    v_ref,
    u_ref,
    t_ref,
    r_ref,
    d_ref,
    v_sem,
    u_sem,
    out_sem,
):
    rows, cols = v_hbm.shape
    blocks = rows // 256
    per = u_low.shape[0]
    u_copies = []
    for n in range(2 * per):
        u, t = (u_low, t_low) if n < per else (u_high, t_high)
        at = n % per
        u_copies.append(
            [
                pltpu.make_async_copy(u.at[at], u_ref.at[n], u_sem.at[0, n]),
                pltpu.make_async_copy(t.at[at], t_ref.at[n], u_sem.at[1, n]),
            ]
        )
    for c in u_copies[0]:
        c.start()
    v_copies, out_copies = [], []
    for b in range(blocks):
        at = pl.ds(b * 256, 256)
        v_copies.append(pltpu.make_async_copy(v_hbm.at[at], v_ref.at[at], v_sem.at[b]))
        out_copies.append(pltpu.make_async_copy(r_ref.at[at], vectors_hbm.at[at], out_sem.at[b]))
    for step in range(2 * per):
        for b in (2 * step, 2 * step + 1):
            if b < blocks:
                v_copies[b].start()
        if step:
            for c in u_copies[step]:
                c.start()
    mix = mix_ref[...]
    weight = weight_ref[...]
    down, along = iota((256, 256), 0), iota((256, 256), 1)
    same_atom = (down % GROUP) == (along % GROUP)
    spread = ((down // GROUP) == (along % NPMAX)).astype(jnp.float32).astype(jnp.bfloat16)
    same_i = (down // GROUP) == (along // NPMAX)

    def rotate(b):
        v_copies[b].wait()
        at = slice(b * 256, (b + 1) * 256)
        panel = jnp.concatenate([own_ref[at, :], other_ref[at, :]], axis=1)
        turned = v_ref[at, :].astype(jnp.float32) - dot(panel, mix, NT)
        r_ref[at, :] = turned.astype(jnp.bfloat16)
        out_copies[b].start()

    def pairs_of(step):
        for c in u_copies[step]:
            c.wait()
        turned = u_ref[step].astype(jnp.float32) - dot(t_ref[step], mix, NT)
        rounded = turned.astype(jnp.bfloat16)
        weighted = (rounded.astype(jnp.float32) * weight).astype(jnp.bfloat16)
        pairs = jnp.where(same_atom, dot(weighted, rounded, NT), 0.0)
        high = pairs.astype(jnp.bfloat16)
        low = (pairs - high.astype(jnp.float32)).astype(jnp.bfloat16)
        spreaded = jnp.where(same_i, dot(high, spread) + dot(low, spread), 0.0)
        total = spreaded[:GROUP]
        for i in range(1, NPMAX):
            total = total + spreaded[i * GROUP : (i + 1) * GROUP]
        return total

    for step in range(2 * per):
        d_ref[step * GROUP : (step + 1) * GROUP, :] = pairs_of(step)
        for b in (2 * step, 2 * step + 1):
            if b < blocks:
                rotate(b)
    mine = pl.multiple_of(col_ref[0] * (per * GROUP), per * GROUP)
    own_out[...] = d_ref[pl.ds(mine, per * GROUP), :]
    other_out[...] = d_ref[pl.ds(per * GROUP - mine, per * GROUP), :]
    for c in out_copies:
        c.wait()


def call(kernel, out_shape, in_specs, out_specs, flops, nbytes, mib, **kw):
    return pl.pallas_call(
        kernel,
        out_shape=out_shape,
        in_specs=in_specs,
        out_specs=out_specs,
        compiler_params=pltpu.CompilerParams(vmem_limit_bytes=mib * MIB),
        cost_estimate=pl.CostEstimate(flops=flops, bytes_accessed=nbytes, transcendentals=0),
        **kw,
    )


def local(
    vectors_in, panel, factor, atom_basis, proj_count, coupling, block_present, occ_mask, occ_weight
):
    rows, cols = vectors_in.shape
    half = panel.shape[1]
    npan = 2 * half
    counts = atom_basis[0]
    atoms = counts.shape[0]
    groups = atoms // GROUP
    n_row = lax.axis_size("row")
    n_col = lax.axis_size("col")
    col = lax.axis_index("col")
    vmem = pl.BlockSpec(memory_space=VM)
    smem = pl.BlockSpec(memory_space=SM)
    hbm = pl.BlockSpec(memory_space=pltpu.MemorySpace.HBM)
    bf16, f32 = jnp.bfloat16, jnp.float32

    other = lax.ppermute(panel, "col", [(0, 1), (1, 0)])
    v_in_hbm = pltpu.with_memory_space_constraint(vectors_in, pltpu.MemorySpace.HBM)

    tile = 256
    partial = pl.pallas_call(
        inner_kernel,
        out_shape=jax.ShapeDtypeStruct((cols, npan), bf16),
        grid=(cols // tile,),
        in_specs=[
            pl.BlockSpec((rows, half), lambda c: (0, 0)),
            pl.BlockSpec((rows, half), lambda c: (0, 0)),
            pl.BlockSpec((rows, tile), lambda c: (0, c)),
        ],
        out_specs=pl.BlockSpec((tile, npan), lambda c: (c, 0)),
        scratch_shapes=[pltpu.VMEM((npan, rows), bf16)],
        compiler_params=pltpu.CompilerParams(vmem_limit_bytes=24 * MIB),
        cost_estimate=pl.CostEstimate(
            flops=2 * rows * cols * npan, bytes_accessed=6 << 20, transcendentals=0
        ),
    )(panel, other, v_in_hbm)
    slices = lax.all_to_all(partial, "row", 0, 0, tiled=True)
    slices = slices.reshape(n_row, cols // n_row, npan)

    to_next, to_last = call(
        halo_kernel,
        [jax.ShapeDtypeStruct((EDGE, cols + npan), bf16)] * 2,
        [smem] + [hbm] * 4,
        [vmem, vmem],
        1 << 26,
        2 << 20,
        16,
        scratch_shapes=[
            pltpu.VMEM((2, TAIL, cols + npan), bf16),
            pltpu.SemaphoreType.DMA((2, 3)),
        ],
    )(counts, v_in_hbm, panel, other, partial)
    up = [(i, (i + 1) % n_row) for i in range(n_row)]
    before = lax.ppermute(to_next, "row", up)
    after = lax.ppermute(to_last, "row", [(j, i) for i, j in up])

    per = groups // 2
    blocks = coupling.transpose(1, 0, 2)
    present = block_present.T
    halves = []
    for n, halo in enumerate((before, after)):
        halves.append(
            call(
                functools.partial(pre_kernel, n * per),
                [
                    pltpu.HBM((per, 256, cols), bf16),
                    pltpu.HBM((per, 256, npan), bf16),
                    jax.ShapeDtypeStruct((1,), jnp.int32),
                ],
                [smem] + [vmem] * 4 + [hbm] * 3,
                [hbm, hbm, smem],
                per * 2 * 256 * WIDE * (WIDE + cols + npan),
                10 << 20,
                28,
                scratch_shapes=[
                    pltpu.SMEM((atoms + 2 * RIM,), jnp.int32),
                    pltpu.VMEM((per, 256, WIDE), bf16),
                    pltpu.VMEM((16, atoms), f32),
                    pltpu.VMEM((atoms, 16), f32),
                    pltpu.VMEM((rows + 2 * EDGE, cols), bf16),
                    pltpu.VMEM((rows + 2 * EDGE, npan), bf16),
                    pltpu.VMEM((per, 256, cols), bf16),
                    pltpu.VMEM((per, 256, npan), bf16),
                    pltpu.SemaphoreType.DMA((3,)),
                    pltpu.SemaphoreType.DMA((2, per)),
                ],
            )(counts, present, proj_count[None, :], blocks, halo, v_in_hbm, panel, other)
        )
    mark = halves[0][2]
    ready = [
        pltpu.with_memory_space_constraint(x, pltpu.MemorySpace.HBM)
        for x in halves[0][:2] + halves[1][:2]
    ]

    flipped = jnp.roll(jnp.roll(factor, half, axis=0), half, axis=1)
    ordered = jnp.where(col == 0, factor, flipped)
    copies = call(
        mix_kernel,
        jax.ShapeDtypeStruct((n_row, cols // n_row, npan), bf16),
        [smem, vmem, vmem],
        vmem,
        1 << 24,
        1 << 20,
        8,
    )(mark, slices, ordered)
    mixing = lax.all_to_all(copies.reshape(cols, npan), "row", 0, 0, tiled=True)

    weights = (occ_mask.astype(f32) * occ_weight / (cols * n_col))[None, :]
    vectors, own_part, other_part = call(
        main_kernel,
        [
            jax.ShapeDtypeStruct((rows, cols), bf16),
            jax.ShapeDtypeStruct((atoms // 2, 256), f32),
            jax.ShapeDtypeStruct((atoms // 2, 256), f32),
        ],
        [smem] + [vmem] * 4 + [hbm] * 5,
        [hbm, vmem, vmem],
        10 << 30,
        14 << 20,
        28,
        scratch_shapes=[
            pltpu.VMEM((rows, cols), bf16),
            pltpu.VMEM((groups, 256, cols), bf16),
            pltpu.VMEM((groups, 256, npan), bf16),
            pltpu.VMEM((rows, cols), bf16),
            pltpu.VMEM((atoms, 256), f32),
            pltpu.SemaphoreType.DMA((rows // 256,)),
            pltpu.SemaphoreType.DMA((2, groups)),
            pltpu.SemaphoreType.DMA((rows // 256,)),
        ],
    )(col[None], mixing, weights, panel, other, *ready, v_in_hbm)
    density = own_part + lax.ppermute(other_part, "col", [(0, 1), (1, 0)])
    return vectors, density


def solution(mesh):
    placed = (
        P("row", "col"),
        P("row", "col"),
        P(),
        P("row", None),
        P("row"),
        P("row", None, None),
        P("row", None),
        P("col"),
        P("col"),
    )
    return jax.shard_map(
        local,
        mesh=mesh,
        in_specs=placed,
        out_specs=(P("row", "col"), P(("row", "col"), None)),
        check_vma=False,
    )
```

```python
import functools

import jax
import jax.numpy as jnp
from jax import lax
from jax.experimental import pallas as pl
from jax.experimental.pallas import tpu as pltpu
from jax.sharding import PartitionSpec as P

NPMAX = 16
BMAX = 24
K = 9
RIM = 4
EDGE = RIM * BMAX
TAIL = 128
GROUP = 16
SPAN = GROUP + 2 * RIM
WIDE = 640
ALIGN = 64
MIB = 1024 * 1024

VM = pltpu.MemorySpace.VMEM
SM = pltpu.MemorySpace.SMEM
NT = (((1,), (1,)), ((), ()))
NN = (((1,), (0,)), ((), ()))


def dot(a, b, dims=NN, **kw):
    return lax.dot_general(a, b, dims, preferred_element_type=jnp.float32, **kw)


def iota(shape, dim):
    return lax.broadcasted_iota(jnp.int32, shape, dim)


def padded_rows(counts_ref, first_atom, first_row, source):
    slot = iota((EDGE, 1), 0)
    target = jnp.full((EDGE, 1), -1, jnp.int32)
    row = first_row
    for t in range(RIM):
        count = counts_ref[first_atom + t]
        u = slot - t * BMAX
        target = jnp.where((u >= 0) & (u < count), row + u, target)
        row = row + count
    pick = (iota((EDGE, TAIL), 1) == target).astype(jnp.float32).astype(jnp.bfloat16)
    return dot(pick, source).astype(jnp.bfloat16)


def halo_kernel(
    counts_ref, v_hbm, own_hbm, other_hbm, partial_hbm, to_next, to_last, rows_ref, sem
):
    atoms = counts_ref.shape[0]
    rows, cols = v_hbm.shape
    half = own_hbm.shape[1]
    spans = ((0, cols), (cols, half), (cols + half, half))
    copies = []
    for n, first in enumerate((0, rows - TAIL)):
        for m, (src, (at, width)) in enumerate(zip((v_hbm, own_hbm, other_hbm), spans)):
            copies.append(
                pltpu.make_async_copy(
                    src.at[pl.ds(first, TAIL)],
                    rows_ref.at[n, :, pl.ds(at, width)],
                    sem.at[n, m],
                )
            )
            copies[-1].start()
    tail = counts_ref[atoms - 1]
    for t in range(1, RIM):
        tail = tail + counts_ref[atoms - 1 - t]
    for c in copies:
        c.wait()
    to_next[...] = padded_rows(counts_ref, atoms - RIM, TAIL - tail, rows_ref[1])
    to_last[...] = padded_rows(counts_ref, 0, 0, rows_ref[0])


def pre_kernel(
    which_groups,
    counts_ref,
    present_ref,
    proj_ref,
    cm_ref,
    before_ref,
    after_ref,
    v_hbm,
    own_hbm,
    other_hbm,
    u_hbm,
    t_hbm,
    mark_ref,
    pos_ref,
    cp_ref,
    mask_ref,
    column_ref,
    e_ref,
    p_ref,
    u_ref,
    t_ref,
    sem,
    out_sem,
):
    atoms = counts_ref.shape[0]
    rows, cols = v_hbm.shape
    half = own_hbm.shape[1]
    inner = pl.ds(EDGE, rows)
    copies = [
        pltpu.make_async_copy(v_hbm, e_ref.at[inner], sem.at[0]),
        pltpu.make_async_copy(own_hbm, p_ref.at[inner, pl.ds(0, half)], sem.at[1]),
        pltpu.make_async_copy(other_hbm, p_ref.at[inner, pl.ds(half, half)], sem.at[2]),
    ]
    for c in copies:
        c.start()
    out_copies = []
    for halo_ref, at in ((before_ref, 0), (after_ref, EDGE + rows)):
        mine = slice(at, at + EDGE)
        if halo_ref is None:
            e_ref[mine, :] = jnp.zeros((EDGE, cols), jnp.bfloat16)
            p_ref[mine, :] = jnp.zeros((EDGE, 2 * half), jnp.bfloat16)
        else:
            e_ref[mine, :] = halo_ref[:, :cols]
            p_ref[mine, :] = halo_ref[:, cols:]
    mark_ref[0] = counts_ref[0]

    for t in range(RIM):
        pos_ref[t] = t * BMAX
        pos_ref[RIM + atoms + t] = EDGE + rows + t * BMAX

    def add(t, at):
        pos_ref[RIM + t] = at
        return at + counts_ref[t]

    lax.fori_loop(0, atoms, add, jnp.int32(EDGE), unroll=8)
    mask_ref[...] = jnp.zeros(mask_ref.shape, jnp.float32)
    mask_ref[:K, :] = present_ref[...].astype(jnp.float32)
    mask_ref[K : K + 1, :] = proj_ref[...].astype(jnp.float32)
    column_ref[...] = mask_ref[...].T
    lanes = NPMAX * BMAX
    lane = iota((8, WIDE), 1)
    which = lane // BMAX
    slot = lane - which * BMAX
    sub = iota((GROUP, lanes), 1) // BMAX
    for n, g in enumerate(which_groups):
        mine = slice(g * GROUP, (g + 1) * GROUP)
        first = pos_ref[g * GROUP]
        start = jnp.minimum((first // ALIGN) * ALIGN, rows + 2 * EDGE - WIDE)
        target = jnp.full((8, WIDE), -1, jnp.int32)
        for t in range(SPAN):
            atom = g * GROUP + t - RIM
            count = counts_ref[atom] if 0 <= atom < atoms else BMAX
            at = pos_ref[atom + RIM] - start
            target = jnp.where((which == t) & (slot < count), at + slot, target)
        pick = (iota((WIDE, WIDE), 0) == target[:1]).astype(jnp.float32).astype(jnp.bfloat16)
        kept = column_ref[mine, K : K + 1] > sub.astype(jnp.float32)
        x = []
        for k in range(K):
            block = cm_ref[k, mine, :].astype(jnp.float32)
            x.append(jnp.where((column_ref[mine, k : k + 1] > 0.0) & kept, block, 0.0))
        x += [None] * (NPMAX - K)
        for bit in (1, 2, 4, 8):
            low = (sub & bit) == 0
            new = list(x)
            for p in range(NPMAX):
                q = p + bit
                if p & bit or (x[p] is None and x[q] is None):
                    continue
                a, b = x[p], x[q]
                zero = jnp.zeros((GROUP, lanes), jnp.float32)
                b_up = zero if b is None else pltpu.roll(b, bit * BMAX, 1)
                a_down = zero if a is None else pltpu.roll(a, lanes - bit * BMAX, 1)
                new[p] = jnp.where(low, zero if a is None else a, b_up)
                new[q] = jnp.where(low, a_down, zero if b is None else b)
            x = new
        pad = jnp.zeros((GROUP, WIDE - lanes), jnp.float32)
        for i in range(NPMAX):
            wide = jnp.concatenate([x[i], pad], axis=1)
            halves = [wide[:8], pltpu.roll(wide[8:], 8 * BMAX, 1)]
            for _ in range(2):
                halves = [pltpu.roll(h, 0, 1, stride=BMAX // 2, stride_axis=0) for h in halves]
            skew = jnp.concatenate(halves, axis=0)
            cp_ref[n, i * GROUP : (i + 1) * GROUP, :] = skew.astype(jnp.bfloat16)
        band = dot(cp_ref[n], pick, NT).astype(jnp.bfloat16)
        if n == 0:
            for c in copies:
                c.wait()
        window = pl.ds(pl.multiple_of(start, ALIGN), WIDE)
        u_ref[n] = dot(band, e_ref[window, :]).astype(jnp.bfloat16)
        t_ref[n] = dot(band, p_ref[window, :]).astype(jnp.bfloat16)
        out_copies.append(pltpu.make_async_copy(u_ref.at[n], u_hbm.at[n], out_sem.at[0, n]))
        out_copies.append(pltpu.make_async_copy(t_ref.at[n], t_hbm.at[n], out_sem.at[1, n]))
        for c in out_copies[-2:]:
            c.start()
    for c in out_copies:
        c.wait()


def own_kernel(own_hbm, v_hbm, done_ref, v_ref, own_ref, acc_ref, sem):
    rows = v_hbm.shape[0]
    blocks = rows // 256
    at = [pl.ds(b * 256, 256) for b in range(blocks)]
    copies = [pltpu.make_async_copy(own_hbm, own_ref, sem.at[blocks])]
    copies += [pltpu.make_async_copy(v_hbm.at[s], v_ref.at[s], sem.at[b]) for b, s in enumerate(at)]
    for c in copies:
        c.start()
    copies[0].wait()
    turned = own_ref[...].T
    for b in range(blocks):
        copies[1 + b].wait()
        mine = slice(b * 256, (b + 1) * 256)
        product = dot(turned[:, mine], v_ref[mine, :])
        acc_ref[...] = product if b == 0 else acc_ref[...] + product
    done_ref[...] = acc_ref[...].T.astype(jnp.bfloat16)


def other_kernel(done_ref, other_ref, v_ref, out_ref):
    half = other_ref.shape[1]
    cols = v_ref.shape[1]
    turned = other_ref[...].T
    out_ref[:, :half] = done_ref[...]
    for at in range(0, cols, 256):
        mine = slice(at, at + 256)
        out_ref[mine, half:] = dot(turned, v_ref[:, mine]).T.astype(jnp.bfloat16)


def mix_kernel(col_ref, mark_ref, parts_ref, factor_ref, out_ref):
    total = jnp.sum(parts_ref[...].astype(jnp.float32), axis=0)
    half = total.shape[1] // 2
    swap = col_ref[0] == 1
    total = jnp.where(swap, pltpu.roll(total, half, 1), total)
    mixed = dot(total, factor_ref[...], precision=lax.Precision.HIGHEST)
    mixed = jnp.where(swap, pltpu.roll(mixed, half, 1), mixed).astype(jnp.bfloat16)
    out_ref[...] = jnp.broadcast_to(mixed[None], out_ref.shape)


def main_kernel(parts, col_ref, mix_ref, weight_ref, own_ref, other_ref, *refs):
    n_parts = len(parts)
    u_hbms, t_hbms = refs[:n_parts], refs[n_parts : 2 * n_parts]
    v_hbm, vectors_hbm, own_out, other_out = refs[2 * n_parts : 2 * n_parts + 4]
    mt_ref, v_ref, u_ref, t_ref, r_ref, d_ref, v_sem, u_sem, out_sem = refs[2 * n_parts + 4 :]
    rows, cols = v_hbm.shape
    blocks = rows // 256
    order = [(g, p, at) for p, part in enumerate(parts) for at, g in enumerate(part)]
    v_copies, out_copies, u_copies = [], [], []
    for b in range(blocks):
        at = pl.ds(b * 256, 256)
        v_copies.append(pltpu.make_async_copy(v_hbm.at[at], v_ref.at[at], v_sem.at[b]))
        out_copies.append(pltpu.make_async_copy(r_ref.at[at], vectors_hbm.at[at], out_sem.at[b]))
    for n, (_, p, at) in enumerate(order):
        u_copies.append(
            [
                pltpu.make_async_copy(u_hbms[p].at[at], u_ref.at[n], u_sem.at[0, n]),
                pltpu.make_async_copy(t_hbms[p].at[at], t_ref.at[n], u_sem.at[1, n]),
            ]
        )
    steps = [(n, [b for b in (2 * n, 2 * n + 1) if b < blocks]) for n in range(len(order))]
    for n, bs in steps:
        for c in u_copies[n] + [v_copies[b] for b in bs]:
            c.start()
    mt_ref[...] = mix_ref[...].T
    mix = mt_ref[...]
    weight = weight_ref[...]
    down, along = iota((256, 256), 0), iota((256, 256), 1)
    same_atom = (down & (GROUP - 1)) == (along & (GROUP - 1))
    spread = ((down >> 4) == (along & (NPMAX - 1))).astype(jnp.float32).astype(jnp.bfloat16)
    same_i = (down >> 4) == (along >> 4)

    def rotate(b):
        v_copies[b].wait()
        at = slice(b * 256, (b + 1) * 256)
        panel = jnp.concatenate([own_ref[at, :], other_ref[at, :]], axis=1)
        turned = v_ref[at, :].astype(jnp.float32) - dot(panel, mix)
        r_ref[at, :] = turned.astype(jnp.bfloat16)
        out_copies[b].start()

    def density_of(n):
        for c in u_copies[n]:
            c.wait()
        turned = u_ref[n].astype(jnp.float32) - dot(t_ref[n], mix)
        rounded = turned.astype(jnp.bfloat16)
        weighted = (rounded.astype(jnp.float32) * weight).astype(jnp.bfloat16)
        pairs = jnp.where(same_atom, dot(weighted, rounded, NT), 0.0)
        high = pairs.astype(jnp.bfloat16)
        low = (pairs - high.astype(jnp.float32)).astype(jnp.bfloat16)
        spreaded = jnp.where(same_i, dot(high, spread) + dot(low, spread), 0.0)
        total = spreaded[:GROUP]
        for i in range(1, NPMAX):
            total = total + spreaded[i * GROUP : (i + 1) * GROUP]
        return total

    for n, bs in steps:
        at = order[n][0] * GROUP
        d_ref[at : at + GROUP, :] = density_of(n)
        for b in bs:
            rotate(b)
    per = own_out.shape[0]
    mine = pl.multiple_of(col_ref[0] * per, per)
    own_out[...] = d_ref[pl.ds(mine, per), :]
    other_out[...] = d_ref[pl.ds(per - mine, per), :]
    for c in out_copies:
        c.wait()


VMEM_SPEC = pl.BlockSpec(memory_space=VM)
SMEM_SPEC = pl.BlockSpec(memory_space=SM)
HBM_SPEC = pl.BlockSpec(memory_space=pltpu.MemorySpace.HBM)
BF16, F32 = jnp.bfloat16, jnp.float32


def in_hbm(x):
    return pltpu.with_memory_space_constraint(x, pltpu.MemorySpace.HBM)


def call(kernel, out_shape, in_specs, out_specs, flops, nbytes, mib, **kw):
    return pl.pallas_call(
        kernel,
        out_shape=out_shape,
        in_specs=in_specs,
        out_specs=out_specs,
        compiler_params=pltpu.CompilerParams(vmem_limit_bytes=mib * MIB),
        cost_estimate=pl.CostEstimate(flops=flops, bytes_accessed=nbytes, transcendentals=0),
        **kw,
    )


def partial_sums(panel, other, v_hbm):
    rows, cols = v_hbm.shape
    half = panel.shape[1]
    work = 2 * rows * cols * half
    done, v_vmem = call(
        own_kernel,
        [pltpu.VMEM((cols, half), BF16), pltpu.VMEM((rows, cols), BF16)],
        [HBM_SPEC, HBM_SPEC],
        [VMEM_SPEC, VMEM_SPEC],
        work,
        5 << 20,
        24,
        scratch_shapes=[
            pltpu.VMEM((rows, half), BF16),
            pltpu.VMEM((half, cols), F32),
            pltpu.SemaphoreType.DMA((rows // 256 + 1,)),
        ],
    )(in_hbm(panel), v_hbm)
    return call(
        other_kernel,
        jax.ShapeDtypeStruct((cols, 2 * half), BF16),
        [VMEM_SPEC] * 3,
        VMEM_SPEC,
        work,
        5 << 20,
        24,
    )(done, other, v_vmem)


def rims(counts, v_hbm, panel, other, partial):
    cols, width = v_hbm.shape[1], v_hbm.shape[1] + 2 * panel.shape[1]
    return call(
        halo_kernel,
        [jax.ShapeDtypeStruct((EDGE, width), BF16)] * 2,
        [SMEM_SPEC] + [HBM_SPEC] * 4,
        [VMEM_SPEC, VMEM_SPEC],
        1 << 26,
        2 << 20,
        16,
        scratch_shapes=[pltpu.VMEM((2, TAIL, width), BF16), pltpu.SemaphoreType.DMA((2, 3))],
    )(counts, v_hbm, panel, other, partial)


def couple(which, counts, present, proj_count, blocks, halos, v_hbm, panel, other):
    rows, cols = v_hbm.shape
    npan = 2 * panel.shape[1]
    atoms = counts.shape[0]
    n = len(which)

    def kernel(counts_ref, present_ref, proj_ref, cm_ref, *rest):
        ends = rest[: len(halos)] if halos else (None, None)
        pre_kernel(which, counts_ref, present_ref, proj_ref, cm_ref, *ends, *rest[len(halos) :])

    return call(
        kernel,
        [
            pltpu.HBM((n, 256, cols), BF16),
            pltpu.HBM((n, 256, npan), BF16),
            jax.ShapeDtypeStruct((1,), jnp.int32),
        ],
        [SMEM_SPEC] + [VMEM_SPEC] * (3 + len(halos)) + [HBM_SPEC] * 3,
        [HBM_SPEC, HBM_SPEC, SMEM_SPEC],
        n * 2 * 256 * WIDE * (WIDE + cols + npan),
        10 << 20,
        28,
        scratch_shapes=[
            pltpu.SMEM((atoms + 2 * RIM,), jnp.int32),
            pltpu.VMEM((n, 256, WIDE), BF16),
            pltpu.VMEM((16, atoms), F32),
            pltpu.VMEM((atoms, 16), F32),
            pltpu.VMEM((rows + 2 * EDGE, cols), BF16),
            pltpu.VMEM((rows + 2 * EDGE, npan), BF16),
            pltpu.VMEM((n, 256, cols), BF16),
            pltpu.VMEM((n, 256, npan), BF16),
            pltpu.SemaphoreType.DMA((3,)),
            pltpu.SemaphoreType.DMA((2, n)),
        ],
    )(counts, present, proj_count, blocks, *halos, v_hbm, panel, other)


def mix(col, mark, slices, factor):
    return call(
        mix_kernel,
        jax.ShapeDtypeStruct(slices.shape, BF16),
        [SMEM_SPEC, SMEM_SPEC, VMEM_SPEC, VMEM_SPEC],
        VMEM_SPEC,
        1 << 24,
        1 << 20,
        8,
    )(col, mark, slices, factor)


def finish(parts, col, mixing, weights, panel, other, us, ts, v_hbm):
    rows, cols = v_hbm.shape
    npan = 2 * panel.shape[1]
    groups = sum(len(p) for p in parts)
    atoms = groups * GROUP
    return call(
        functools.partial(main_kernel, parts),
        [
            jax.ShapeDtypeStruct((rows, cols), BF16),
            jax.ShapeDtypeStruct((atoms // 2, 256), F32),
            jax.ShapeDtypeStruct((atoms // 2, 256), F32),
        ],
        [SMEM_SPEC] + [VMEM_SPEC] * 4 + [HBM_SPEC] * (2 * len(parts) + 1),
        [HBM_SPEC, VMEM_SPEC, VMEM_SPEC],
        6 << 30,
        14 << 20,
        28,
        scratch_shapes=[
            pltpu.VMEM((npan, cols), BF16),
            pltpu.VMEM((rows, cols), BF16),
            pltpu.VMEM((groups, 256, cols), BF16),
            pltpu.VMEM((groups, 256, npan), BF16),
            pltpu.VMEM((rows, cols), BF16),
            pltpu.VMEM((atoms, 256), F32),
            pltpu.SemaphoreType.DMA((rows // 256,)),
            pltpu.SemaphoreType.DMA((2, groups)),
            pltpu.SemaphoreType.DMA((rows // 256,)),
        ],
    )(col, mixing, weights, panel, other, *us, *ts, v_hbm)


def local(
    vectors_in, panel, factor, atom_basis, proj_count, coupling, block_present, occ_mask, occ_weight
):
    cols = vectors_in.shape[1]
    npan = 2 * panel.shape[1]
    counts = atom_basis[0]
    groups = counts.shape[0] // GROUP
    n_row = lax.axis_size("row")
    n_col = lax.axis_size("col")
    col = lax.axis_index("col")[None]
    v_hbm = in_hbm(vectors_in)

    other = lax.ppermute(panel, "col", [(0, 1), (1, 0)])
    partial = partial_sums(panel, other, v_hbm)
    slices = lax.all_to_all(partial, "row", 0, 0, tiled=True)
    slices = slices.reshape(n_row, cols // n_row, npan)

    to_next, to_last = rims(counts, v_hbm, panel, other, partial)
    up = [(i, (i + 1) % n_row) for i in range(n_row)]
    before = lax.ppermute(to_next, "row", up)
    after = lax.ppermute(to_last, "row", [(j, i) for i, j in up])

    early = list(range(1, groups // 2))
    late = list(range(groups // 2, groups)) + [0]
    shared = (counts, block_present.T, proj_count[None, :], coupling.transpose(1, 0, 2))
    u_early, t_early, mark = couple(early, *shared, (), v_hbm, panel, other)
    copies = mix(col, mark, slices, factor)
    mixing = lax.all_to_all(copies.reshape(cols, npan), "row", 0, 0, tiled=True)
    u_late, t_late, _ = couple(late, *shared, (before, after), v_hbm, panel, other)

    weights = (occ_mask.astype(F32) * occ_weight / (cols * n_col))[None, :]
    us, ts = [in_hbm(u_early), in_hbm(u_late)], [in_hbm(t_early), in_hbm(t_late)]
    vectors, own_part, other_part = finish(
        (early, late), col, mixing, weights, panel, other, us, ts, v_hbm
    )
    density = own_part + lax.ppermute(other_part, "col", [(0, 1), (1, 0)])
    return vectors, density


def solution(mesh):
    placed = (
        P("row", "col"),
        P("row", "col"),
        P(),
        P("row", None),
        P("row"),
        P("row", None, None),
        P("row", None),
        P("col"),
        P("col"),
    )
    return jax.shard_map(
        local,
        mesh=mesh,
        in_specs=placed,
        out_specs=(P("row", "col"), P(("row", "col"), None)),
        check_vma=False,
    )
```

```python
import functools

import jax
import jax.numpy as jnp
from jax import lax
from jax.experimental import pallas as pl
from jax.experimental.pallas import tpu as pltpu
from jax.sharding import PartitionSpec as P

NPMAX = 16
BMAX = 24
K = 9
RIM = 4
EDGE = RIM * BMAX
TAIL = 128
GROUP = 16
SPAN = GROUP + 2 * RIM
WIDE = 640
ALIGN = 64
MIB = 1024 * 1024

VM = pltpu.MemorySpace.VMEM
SM = pltpu.MemorySpace.SMEM
NT = (((1,), (1,)), ((), ()))
NN = (((1,), (0,)), ((), ()))


def dot(a, b, dims=NN, **kw):
    return lax.dot_general(a, b, dims, preferred_element_type=jnp.float32, **kw)


def iota(shape, dim):
    return lax.broadcasted_iota(jnp.int32, shape, dim)


def padded_rows(counts_ref, first_atom, first_row, sources):
    slot = iota((EDGE, 1), 0)
    target = jnp.full((EDGE, 1), -1, jnp.int32)
    row = first_row
    for t in range(RIM):
        count = counts_ref[first_atom + t]
        u = slot - t * BMAX
        target = jnp.where((u >= 0) & (u < count), row + u, target)
        row = row + count
    pick = (iota((EDGE, TAIL), 1) == target).astype(jnp.float32).astype(jnp.bfloat16)
    return [dot(pick, source).astype(jnp.bfloat16) for source in sources]


def fill_rims(counts_ref, e_ref, p_ref, to_next, to_last):
    atoms = counts_ref.shape[0]
    cols = e_ref.shape[1]
    end = e_ref.shape[0] - EDGE
    tail = counts_ref[atoms - 1]
    for t in range(1, RIM):
        tail = tail + counts_ref[atoms - 1 - t]
    for out, atom, row, at in (
        (to_next, atoms - RIM, TAIL - tail, slice(end - TAIL, end)),
        (to_last, 0, 0, slice(EDGE, EDGE + TAIL)),
    ):
        pieces = padded_rows(counts_ref, atom, row, [e_ref[at, :], p_ref[at, :]])
        out[:, :cols] = pieces[0]
        out[:, cols:] = pieces[1]


def pre_kernel(
    which_groups,
    rim_refs,
    counts_ref,
    present_ref,
    proj_ref,
    cm_ref,
    before_ref,
    after_ref,
    v_hbm,
    own_hbm,
    other_hbm,
    u_hbm,
    t_hbm,
    mark_ref,
    pos_ref,
    cp_ref,
    mask_ref,
    column_ref,
    e_ref,
    p_ref,
    u_ref,
    t_ref,
    sem,
    out_sem,
):
    atoms = counts_ref.shape[0]
    rows, cols = v_hbm.shape
    half = own_hbm.shape[1]
    inner = pl.ds(EDGE, rows)
    copies = [
        pltpu.make_async_copy(v_hbm, e_ref.at[inner], sem.at[0]),
        pltpu.make_async_copy(own_hbm, p_ref.at[inner, pl.ds(0, half)], sem.at[1]),
        pltpu.make_async_copy(other_hbm, p_ref.at[inner, pl.ds(half, half)], sem.at[2]),
    ]
    for c in copies:
        c.start()
    out_copies = []
    for halo_ref, at in ((before_ref, 0), (after_ref, EDGE + rows)):
        mine = slice(at, at + EDGE)
        if halo_ref is None:
            e_ref[mine, :] = jnp.zeros((EDGE, cols), jnp.bfloat16)
            p_ref[mine, :] = jnp.zeros((EDGE, 2 * half), jnp.bfloat16)
        else:
            e_ref[mine, :] = halo_ref[:, :cols]
            p_ref[mine, :] = halo_ref[:, cols:]
    mark_ref[0] = counts_ref[0]

    for t in range(RIM):
        pos_ref[t] = t * BMAX
        pos_ref[RIM + atoms + t] = EDGE + rows + t * BMAX

    def add(t, at):
        pos_ref[RIM + t] = at
        return at + counts_ref[t]

    lax.fori_loop(0, atoms, add, jnp.int32(EDGE), unroll=8)
    mask_ref[...] = jnp.zeros(mask_ref.shape, jnp.float32)
    mask_ref[:K, :] = present_ref[...].astype(jnp.float32)
    mask_ref[K : K + 1, :] = proj_ref[...].astype(jnp.float32)
    column_ref[...] = mask_ref[...].T
    lanes = NPMAX * BMAX
    lane = iota((8, WIDE), 1)
    which = lane // BMAX
    slot = lane - which * BMAX
    sub = iota((GROUP, lanes), 1) // BMAX
    starts, bands = [], []

    def multiply(n):
        if n == 0:
            for c in copies:
                c.wait()
            if rim_refs is not None:
                fill_rims(counts_ref, e_ref, p_ref, *rim_refs)
        window = pl.ds(pl.multiple_of(starts[n], ALIGN), WIDE)
        u_ref[n] = dot(bands[n], e_ref[window, :]).astype(jnp.bfloat16)
        t_ref[n] = dot(bands[n], p_ref[window, :]).astype(jnp.bfloat16)
        out_copies.append(pltpu.make_async_copy(u_ref.at[n], u_hbm.at[n], out_sem.at[0, n]))
        out_copies.append(pltpu.make_async_copy(t_ref.at[n], t_hbm.at[n], out_sem.at[1, n]))
        for c in out_copies[-2:]:
            c.start()

    for n, g in enumerate(which_groups):
        mine = slice(g * GROUP, (g + 1) * GROUP)
        first = pos_ref[g * GROUP]
        start = jnp.minimum((first // ALIGN) * ALIGN, rows + 2 * EDGE - WIDE)
        target = jnp.full((8, WIDE), -1, jnp.int32)
        for t in range(SPAN):
            atom = g * GROUP + t - RIM
            count = counts_ref[atom] if 0 <= atom < atoms else BMAX
            at = pos_ref[atom + RIM] - start
            target = jnp.where((which == t) & (slot < count), at + slot, target)
        pick = (iota((WIDE, WIDE), 0) == target[:1]).astype(jnp.float32).astype(jnp.bfloat16)
        kept = column_ref[mine, K : K + 1] > sub.astype(jnp.float32)
        x = []
        for k in range(K):
            block = cm_ref[k, mine, :].astype(jnp.float32)
            x.append(jnp.where((column_ref[mine, k : k + 1] > 0.0) & kept, block, 0.0))
        x += [None] * (NPMAX - K)
        for bit in (1, 2, 4, 8):
            low = (sub & bit) == 0
            new = list(x)
            for p in range(NPMAX):
                q = p + bit
                if p & bit or (x[p] is None and x[q] is None):
                    continue
                a, b = x[p], x[q]
                zero = jnp.zeros((GROUP, lanes), jnp.float32)
                b_up = zero if b is None else pltpu.roll(b, bit * BMAX, 1)
                a_down = zero if a is None else pltpu.roll(a, lanes - bit * BMAX, 1)
                new[p] = jnp.where(low, zero if a is None else a, b_up)
                new[q] = jnp.where(low, a_down, zero if b is None else b)
            x = new
        pad = jnp.zeros((GROUP, WIDE - lanes), jnp.float32)
        for i in range(NPMAX):
            wide = jnp.concatenate([x[i], pad], axis=1)
            halves = [wide[:8], pltpu.roll(wide[8:], 8 * BMAX, 1)]
            for _ in range(2):
                halves = [pltpu.roll(h, 0, 1, stride=BMAX // 2, stride_axis=0) for h in halves]
            skew = jnp.concatenate(halves, axis=0)
            cp_ref[n, i * GROUP : (i + 1) * GROUP, :] = skew.astype(jnp.bfloat16)
        bands.append(dot(cp_ref[n], pick, NT).astype(jnp.bfloat16))
        starts.append(start)
        multiply(n)
    for c in out_copies:
        c.wait()


def own_kernel(own_hbm, v_hbm, done_ref, v_ref, own_ref, acc_ref, sem):
    rows = v_hbm.shape[0]
    blocks = rows // 256
    at = [pl.ds(b * 256, 256) for b in range(blocks)]
    copies = [pltpu.make_async_copy(own_hbm, own_ref, sem.at[blocks])]
    copies += [pltpu.make_async_copy(v_hbm.at[s], v_ref.at[s], sem.at[b]) for b, s in enumerate(at)]
    for c in copies:
        c.start()
    copies[0].wait()
    turned = own_ref[...].T
    for b in range(blocks):
        copies[1 + b].wait()
        mine = slice(b * 256, (b + 1) * 256)
        product = dot(turned[:, mine], v_ref[mine, :])
        acc_ref[...] = product if b == 0 else acc_ref[...] + product
    done_ref[...] = acc_ref[...].T.astype(jnp.bfloat16)


def other_kernel(done_ref, other_ref, v_ref, out_ref):
    half = other_ref.shape[1]
    cols = v_ref.shape[1]
    turned = other_ref[...].T
    out_ref[:, :half] = done_ref[...]
    for at in range(0, cols, 256):
        mine = slice(at, at + 256)
        out_ref[mine, half:] = dot(turned, v_ref[:, mine]).T.astype(jnp.bfloat16)


def mix_kernel(col_ref, mark_ref, parts_ref, factor_ref, rim_ref, out_ref, rim_out, sem):
    passing = pltpu.make_async_copy(rim_ref, rim_out, sem)
    passing.start()
    total = jnp.sum(parts_ref[...].astype(jnp.float32), axis=0)
    half = total.shape[1] // 2
    swap = col_ref[0] == 1
    total = jnp.where(swap, pltpu.roll(total, half, 1), total)
    mixed = dot(total, factor_ref[...], precision=lax.Precision.HIGHEST)
    mixed = jnp.where(swap, pltpu.roll(mixed, half, 1), mixed).astype(jnp.bfloat16)
    out_ref[...] = jnp.broadcast_to(mixed[None], out_ref.shape)
    passing.wait()


def main_kernel(parts, col_ref, mix_ref, weight_ref, own_ref, other_ref, *refs):
    n_parts = len(parts)
    u_hbms, t_hbms = refs[:n_parts], refs[n_parts : 2 * n_parts]
    v_hbm, vectors_hbm, own_out, other_out = refs[2 * n_parts : 2 * n_parts + 4]
    mt_ref, v_ref, u_ref, t_ref, r_ref, d_ref, v_sem, u_sem, out_sem = refs[2 * n_parts + 4 :]
    rows, cols = v_hbm.shape
    blocks = rows // 256
    order = [(g, p, at) for p, part in enumerate(parts) for at, g in enumerate(part)]
    v_copies, out_copies, u_copies = [], [], []
    for b in range(blocks):
        at = pl.ds(b * 256, 256)
        v_copies.append(pltpu.make_async_copy(v_hbm.at[at], v_ref.at[at], v_sem.at[b]))
        out_copies.append(pltpu.make_async_copy(r_ref.at[at], vectors_hbm.at[at], out_sem.at[b]))
    for n, (_, p, at) in enumerate(order):
        u_copies.append(
            [
                pltpu.make_async_copy(u_hbms[p].at[at], u_ref.at[n], u_sem.at[0, n]),
                pltpu.make_async_copy(t_hbms[p].at[at], t_ref.at[n], u_sem.at[1, n]),
            ]
        )
    steps = [(n, [b for b in (2 * n, 2 * n + 1) if b < blocks]) for n in range(len(order))]
    for n, bs in steps:
        for c in u_copies[n] + [v_copies[b] for b in bs]:
            c.start()
    mt_ref[...] = mix_ref[...].T
    mix = mt_ref[...]
    weight = weight_ref[...]
    down, along = iota((256, 256), 0), iota((256, 256), 1)
    same_atom = (down & (GROUP - 1)) == (along & (GROUP - 1))
    spread = ((down >> 4) == (along & (NPMAX - 1))).astype(jnp.float32).astype(jnp.bfloat16)
    same_i = (down >> 4) == (along >> 4)

    def rotate(b):
        v_copies[b].wait()
        at = slice(b * 256, (b + 1) * 256)
        panel = jnp.concatenate([own_ref[at, :], other_ref[at, :]], axis=1)
        turned = v_ref[at, :].astype(jnp.float32) - dot(panel, mix)
        r_ref[at, :] = turned.astype(jnp.bfloat16)
        out_copies[b].start()

    def density_of(n):
        for c in u_copies[n]:
            c.wait()
        turned = u_ref[n].astype(jnp.float32) - dot(t_ref[n], mix)
        rounded = turned.astype(jnp.bfloat16)
        weighted = (rounded.astype(jnp.float32) * weight).astype(jnp.bfloat16)
        pairs = jnp.where(same_atom, dot(weighted, rounded, NT), 0.0)
        high = pairs.astype(jnp.bfloat16)
        low = (pairs - high.astype(jnp.float32)).astype(jnp.bfloat16)
        spreaded = jnp.where(same_i, dot(high, spread) + dot(low, spread), 0.0)
        total = spreaded[:GROUP]
        for i in range(1, NPMAX):
            total = total + spreaded[i * GROUP : (i + 1) * GROUP]
        return total

    for n, bs in steps:
        at = order[n][0] * GROUP
        d_ref[at : at + GROUP, :] = density_of(n)
        for b in bs:
            rotate(b)
    per = own_out.shape[0]
    mine = pl.multiple_of(col_ref[0] * per, per)
    own_out[...] = d_ref[pl.ds(mine, per), :]
    other_out[...] = d_ref[pl.ds(per - mine, per), :]
    for c in out_copies:
        c.wait()


VMEM_SPEC = pl.BlockSpec(memory_space=VM)
SMEM_SPEC = pl.BlockSpec(memory_space=SM)
HBM_SPEC = pl.BlockSpec(memory_space=pltpu.MemorySpace.HBM)
BF16, F32 = jnp.bfloat16, jnp.float32


def in_hbm(x):
    return pltpu.with_memory_space_constraint(x, pltpu.MemorySpace.HBM)


def call(kernel, out_shape, in_specs, out_specs, flops, nbytes, mib, **kw):
    return pl.pallas_call(
        kernel,
        out_shape=out_shape,
        in_specs=in_specs,
        out_specs=out_specs,
        compiler_params=pltpu.CompilerParams(vmem_limit_bytes=mib * MIB),
        cost_estimate=pl.CostEstimate(flops=flops, bytes_accessed=nbytes, transcendentals=0),
        **kw,
    )


def partial_sums(panel, other, v_hbm):
    rows, cols = v_hbm.shape
    half = panel.shape[1]
    work = 2 * rows * cols * half
    done, v_vmem = call(
        own_kernel,
        [pltpu.VMEM((cols, half), BF16), pltpu.VMEM((rows, cols), BF16)],
        [HBM_SPEC, HBM_SPEC],
        [VMEM_SPEC, VMEM_SPEC],
        work,
        5 << 20,
        24,
        scratch_shapes=[
            pltpu.VMEM((rows, half), BF16),
            pltpu.VMEM((half, cols), F32),
            pltpu.SemaphoreType.DMA((rows // 256 + 1,)),
        ],
    )(in_hbm(panel), v_hbm)
    return call(
        other_kernel,
        pltpu.VMEM((cols, 2 * half), BF16),
        [VMEM_SPEC] * 3,
        VMEM_SPEC,
        work,
        5 << 20,
        24,
    )(done, other, v_vmem)


def couple(which, counts, present, proj_count, blocks, halos, v_hbm, panel, other):
    rows, cols = v_hbm.shape
    npan = 2 * panel.shape[1]
    atoms = counts.shape[0]
    n = len(which)

    first = not halos

    def kernel(counts_ref, present_ref, proj_ref, cm_ref, *rest):
        ends = (None, None) if first else rest[:2]
        rest = rest[len(halos) :]
        rim_refs = rest[6:8] if first else None
        rest = rest[:6] + rest[8:] if first else rest
        pre_kernel(which, rim_refs, counts_ref, present_ref, proj_ref, cm_ref, *ends, *rest)

    return call(
        kernel,
        [
            pltpu.HBM((n, 256, cols), BF16),
            pltpu.HBM((n, 256, npan), BF16),
            jax.ShapeDtypeStruct((1,), jnp.int32),
        ]
        + [jax.ShapeDtypeStruct((EDGE, cols + npan), BF16)] * (2 if first else 0),
        [SMEM_SPEC] + [VMEM_SPEC] * (3 + len(halos)) + [HBM_SPEC] * 3,
        [HBM_SPEC, HBM_SPEC, SMEM_SPEC] + [VMEM_SPEC] * (2 if first else 0),
        n * 2 * 256 * WIDE * (WIDE + cols + npan),
        10 << 20,
        28,
        scratch_shapes=[
            pltpu.SMEM((atoms + 2 * RIM,), jnp.int32),
            pltpu.VMEM((n, 256, WIDE), BF16),
            pltpu.VMEM((16, atoms), F32),
            pltpu.VMEM((atoms, 16), F32),
            pltpu.VMEM((rows + 2 * EDGE, cols), BF16),
            pltpu.VMEM((rows + 2 * EDGE, npan), BF16),
            pltpu.VMEM((n, 256, cols), BF16),
            pltpu.VMEM((n, 256, npan), BF16),
            pltpu.SemaphoreType.DMA((3,)),
            pltpu.SemaphoreType.DMA((2, n)),
        ],
    )(counts, present, proj_count, blocks, *halos, v_hbm, panel, other)


def mix(col, mark, slices, factor, rim):
    return call(
        mix_kernel,
        [pltpu.VMEM(slices.shape, BF16), pltpu.VMEM(rim.shape, BF16)],
        [SMEM_SPEC, SMEM_SPEC, VMEM_SPEC, VMEM_SPEC, VMEM_SPEC],
        [VMEM_SPEC, VMEM_SPEC],
        1 << 24,
        1 << 20,
        8,
        scratch_shapes=[pltpu.SemaphoreType.DMA],
    )(col, mark, slices, factor, rim)


def finish(parts, col, mixing, weights, panel, other, us, ts, v_hbm):
    rows, cols = v_hbm.shape
    npan = 2 * panel.shape[1]
    groups = sum(len(p) for p in parts)
    atoms = groups * GROUP
    return call(
        functools.partial(main_kernel, parts),
        [
            jax.ShapeDtypeStruct((rows, cols), BF16),
            jax.ShapeDtypeStruct((atoms // 2, 256), F32),
            jax.ShapeDtypeStruct((atoms // 2, 256), F32),
        ],
        [SMEM_SPEC] + [VMEM_SPEC] * 4 + [HBM_SPEC] * (2 * len(parts) + 1),
        [HBM_SPEC, VMEM_SPEC, VMEM_SPEC],
        6 << 30,
        14 << 20,
        28,
        scratch_shapes=[
            pltpu.VMEM((npan, cols), BF16),
            pltpu.VMEM((rows, cols), BF16),
            pltpu.VMEM((groups, 256, cols), BF16),
            pltpu.VMEM((groups, 256, npan), BF16),
            pltpu.VMEM((rows, cols), BF16),
            pltpu.VMEM((atoms, 256), F32),
            pltpu.SemaphoreType.DMA((rows // 256,)),
            pltpu.SemaphoreType.DMA((2, groups)),
            pltpu.SemaphoreType.DMA((rows // 256,)),
        ],
    )(col, mixing, weights, panel, other, *us, *ts, v_hbm)


def local(
    vectors_in, panel, factor, atom_basis, proj_count, coupling, block_present, occ_mask, occ_weight
):
    cols = vectors_in.shape[1]
    npan = 2 * panel.shape[1]
    counts = atom_basis[0]
    groups = counts.shape[0] // GROUP
    n_row = lax.axis_size("row")
    n_col = lax.axis_size("col")
    col = lax.axis_index("col")[None]
    v_hbm = in_hbm(vectors_in)

    other = lax.ppermute(panel, "col", [(0, 1), (1, 0)])
    partial = partial_sums(panel, other, v_hbm)
    slices = lax.all_to_all(partial, "row", 0, 0, tiled=True)
    slices = slices.reshape(n_row, cols // n_row, npan)

    early = list(range(1, groups // 2))
    late = list(range(groups // 2, groups)) + [0]
    shared = (counts, block_present.T, proj_count[None, :], coupling.transpose(1, 0, 2))
    u_early, t_early, mark, to_next, to_last = couple(early, *shared, (), v_hbm, panel, other)
    up = [(i, (i + 1) % n_row) for i in range(n_row)]
    before = lax.ppermute(to_next, "row", up)
    copies, to_last = mix(col, mark, slices, factor, to_last)
    after = lax.ppermute(to_last, "row", [(j, i) for i, j in up])
    mixing = lax.all_to_all(copies.reshape(cols, npan), "row", 0, 0, tiled=True)
    u_late, t_late, _ = couple(late, *shared, (before, after), v_hbm, panel, other)

    weights = (occ_mask.astype(F32) * occ_weight / (cols * n_col))[None, :]
    us, ts = [in_hbm(u_early), in_hbm(u_late)], [in_hbm(t_early), in_hbm(t_late)]
    vectors, own_part, other_part = finish(
        (early, late), col, mixing, weights, panel, other, us, ts, v_hbm
    )
    density = own_part + lax.ppermute(other_part, "col", [(0, 1), (1, 0)])
    return vectors, density


def solution(mesh):
    placed = (
        P("row", "col"),
        P("row", "col"),
        P(),
        P("row", None),
        P("row"),
        P("row", None, None),
        P("row", None),
        P("col"),
        P("col"),
    )
    return jax.shard_map(
        local,
        mesh=mesh,
        in_specs=placed,
        out_specs=(P("row", "col"), P(("row", "col"), None)),
        check_vma=False,
    )
```

```python
import functools

import jax
import jax.numpy as jnp
from jax import lax
from jax.experimental import pallas as pl
from jax.experimental.pallas import tpu as pltpu
from jax.sharding import PartitionSpec as P

NPMAX = 16
BMAX = 24
K = 9
RIM = 4
EDGE = RIM * BMAX
TAIL = 128
GROUP = 16
SPAN = GROUP + 2 * RIM
WIDE = 640
ALIGN = 64
MIB = 1024 * 1024

VM = pltpu.MemorySpace.VMEM
SM = pltpu.MemorySpace.SMEM
NT = (((1,), (1,)), ((), ()))
NN = (((1,), (0,)), ((), ()))


def dot(a, b, dims=NN, **kw):
    return lax.dot_general(a, b, dims, preferred_element_type=jnp.float32, **kw)


def iota(shape, dim):
    return lax.broadcasted_iota(jnp.int32, shape, dim)


def padded_rows(counts_ref, first_atom, first_row, sources):
    slot = iota((EDGE, 1), 0)
    target = jnp.full((EDGE, 1), -1, jnp.int32)
    row = first_row
    for t in range(RIM):
        count = counts_ref[first_atom + t]
        u = slot - t * BMAX
        target = jnp.where((u >= 0) & (u < count), row + u, target)
        row = row + count
    pick = (iota((EDGE, TAIL), 1) == target).astype(jnp.float32).astype(jnp.bfloat16)
    return [dot(pick, source).astype(jnp.bfloat16) for source in sources]


def fill_rims(counts_ref, e_ref, p_ref, to_next, to_last):
    atoms = counts_ref.shape[0]
    cols = e_ref.shape[1]
    end = e_ref.shape[0] - EDGE
    tail = counts_ref[atoms - 1]
    for t in range(1, RIM):
        tail = tail + counts_ref[atoms - 1 - t]
    for out, atom, row, at in (
        (to_next, atoms - RIM, TAIL - tail, slice(end - TAIL, end)),
        (to_last, 0, 0, slice(EDGE, EDGE + TAIL)),
    ):
        pieces = padded_rows(counts_ref, atom, row, [e_ref[at, :], p_ref[at, :]])
        out[:, :cols] = pieces[0]
        out[:, cols:] = pieces[1]


def pre_kernel(
    which_groups,
    rim_refs,
    counts_ref,
    present_ref,
    proj_ref,
    cm_ref,
    before_ref,
    after_ref,
    v_hbm,
    own_hbm,
    other_hbm,
    u_hbm,
    t_hbm,
    mark_ref,
    pos_ref,
    cp_ref,
    mask_ref,
    column_ref,
    e_ref,
    p_ref,
    u_ref,
    t_ref,
    sem,
    out_sem,
):
    atoms = counts_ref.shape[0]
    rows, cols = v_hbm.shape
    half = own_hbm.shape[1]
    inner = pl.ds(EDGE, rows)
    copies = [
        pltpu.make_async_copy(v_hbm, e_ref.at[inner], sem.at[0]),
        pltpu.make_async_copy(own_hbm, p_ref.at[inner, pl.ds(0, half)], sem.at[1]),
        pltpu.make_async_copy(other_hbm, p_ref.at[inner, pl.ds(half, half)], sem.at[2]),
    ]
    for c in copies:
        c.start()
    out_copies = []
    for halo_ref, at in ((before_ref, 0), (after_ref, EDGE + rows)):
        mine = slice(at, at + EDGE)
        if halo_ref is None:
            e_ref[mine, :] = jnp.zeros((EDGE, cols), jnp.bfloat16)
            p_ref[mine, :] = jnp.zeros((EDGE, 2 * half), jnp.bfloat16)
        else:
            e_ref[mine, :] = halo_ref[:, :cols]
            p_ref[mine, :] = halo_ref[:, cols:]
    mark_ref[0] = counts_ref[0]

    for t in range(RIM):
        pos_ref[t] = t * BMAX
        pos_ref[RIM + atoms + t] = EDGE + rows + t * BMAX

    def add(t, at):
        pos_ref[RIM + t] = at
        return at + counts_ref[t]

    lax.fori_loop(0, atoms, add, jnp.int32(EDGE), unroll=8)
    mask_ref[...] = jnp.zeros(mask_ref.shape, jnp.float32)
    mask_ref[:K, :] = present_ref[...].astype(jnp.float32)
    mask_ref[K : K + 1, :] = proj_ref[...].astype(jnp.float32)
    column_ref[...] = mask_ref[...].T
    lanes = NPMAX * BMAX
    lane = iota((8, WIDE), 1)
    which = lane // BMAX
    slot = lane - which * BMAX
    sub = iota((GROUP, lanes), 1) // BMAX
    starts, bands = [], []

    def multiply(n):
        if n == 0:
            for c in copies:
                c.wait()
            if rim_refs is not None:
                fill_rims(counts_ref, e_ref, p_ref, *rim_refs)
        window = pl.ds(pl.multiple_of(starts[n], ALIGN), WIDE)
        u_ref[n] = dot(bands[n], e_ref[window, :]).astype(jnp.bfloat16)
        t_ref[n] = dot(bands[n], p_ref[window, :]).astype(jnp.bfloat16)
        out_copies.append(pltpu.make_async_copy(u_ref.at[n], u_hbm.at[n], out_sem.at[0, n]))
        out_copies.append(pltpu.make_async_copy(t_ref.at[n], t_hbm.at[n], out_sem.at[1, n]))
        for c in out_copies[-2:]:
            c.start()

    for n, g in enumerate(which_groups):
        mine = slice(g * GROUP, (g + 1) * GROUP)
        first = pos_ref[g * GROUP]
        start = jnp.minimum((first // ALIGN) * ALIGN, rows + 2 * EDGE - WIDE)
        target = jnp.full((8, WIDE), -1, jnp.int32)
        for t in range(SPAN):
            atom = g * GROUP + t - RIM
            count = counts_ref[atom] if 0 <= atom < atoms else BMAX
            at = pos_ref[atom + RIM] - start
            target = jnp.where((which == t) & (slot < count), at + slot, target)
        pick = (iota((WIDE, WIDE), 0) == target[:1]).astype(jnp.float32).astype(jnp.bfloat16)
        kept = column_ref[mine, K : K + 1] > sub.astype(jnp.float32)
        x = []
        for k in range(K):
            block = cm_ref[k, mine, :].astype(jnp.float32)
            x.append(jnp.where((column_ref[mine, k : k + 1] > 0.0) & kept, block, 0.0))
        x += [None] * (NPMAX - K)
        for bit in (1, 2, 4, 8):
            low = (sub & bit) == 0
            new = list(x)
            for p in range(NPMAX):
                q = p + bit
                if p & bit or (x[p] is None and x[q] is None):
                    continue
                a, b = x[p], x[q]
                zero = jnp.zeros((GROUP, lanes), jnp.float32)
                b_up = zero if b is None else pltpu.roll(b, bit * BMAX, 1)
                a_down = zero if a is None else pltpu.roll(a, lanes - bit * BMAX, 1)
                new[p] = jnp.where(low, zero if a is None else a, b_up)
                new[q] = jnp.where(low, a_down, zero if b is None else b)
            x = new
        pad = jnp.zeros((GROUP, WIDE - lanes), jnp.float32)
        for i in range(NPMAX):
            wide = jnp.concatenate([x[i], pad], axis=1)
            halves = [wide[:8], pltpu.roll(wide[8:], 8 * BMAX, 1)]
            for _ in range(2):
                halves = [pltpu.roll(h, 0, 1, stride=BMAX // 2, stride_axis=0) for h in halves]
            skew = jnp.concatenate(halves, axis=0)
            cp_ref[n, i * GROUP : (i + 1) * GROUP, :] = skew.astype(jnp.bfloat16)
        bands.append(dot(cp_ref[n], pick, NT).astype(jnp.bfloat16))
        starts.append(start)
        multiply(n)
    for c in out_copies:
        c.wait()


def own_kernel(own_hbm, v_hbm, done_ref, v_ref, own_ref, acc_ref, sem):
    rows = v_hbm.shape[0]
    blocks = rows // 256
    at = [pl.ds(b * 256, 256) for b in range(blocks)]
    copies = [pltpu.make_async_copy(own_hbm, own_ref, sem.at[blocks])]
    copies += [pltpu.make_async_copy(v_hbm.at[s], v_ref.at[s], sem.at[b]) for b, s in enumerate(at)]
    for c in copies:
        c.start()
    copies[0].wait()
    turned = own_ref[...].T
    for b in range(blocks):
        copies[1 + b].wait()
        mine = slice(b * 256, (b + 1) * 256)
        product = dot(turned[:, mine], v_ref[mine, :])
        acc_ref[...] = product if b == 0 else acc_ref[...] + product
    done_ref[...] = acc_ref[...].T.astype(jnp.bfloat16)


def other_kernel(done_ref, other_ref, v_ref, out_ref):
    half = other_ref.shape[1]
    cols = v_ref.shape[1]
    turned = other_ref[...].T
    out_ref[:, :half] = done_ref[...]
    for at in range(0, cols, 256):
        mine = slice(at, at + 256)
        out_ref[mine, half:] = dot(turned, v_ref[:, mine]).T.astype(jnp.bfloat16)


def mix_kernel(col_ref, mark_ref, parts_ref, factor_ref, out_ref):
    total = jnp.sum(parts_ref[...].astype(jnp.float32), axis=0)
    half = total.shape[1] // 2
    swap = col_ref[0] == 1
    total = jnp.where(swap, pltpu.roll(total, half, 1), total)
    mixed = dot(total, factor_ref[...], precision=lax.Precision.HIGHEST)
    mixed = jnp.where(swap, pltpu.roll(mixed, half, 1), mixed).astype(jnp.bfloat16)
    out_ref[...] = jnp.broadcast_to(mixed[None], out_ref.shape)


def main_kernel(parts, col_ref, mix_ref, weight_ref, own_ref, other_ref, *refs):
    n_parts = len(parts)
    u_hbms, t_hbms = refs[:n_parts], refs[n_parts : 2 * n_parts]
    v_hbm, vectors_hbm, own_out, other_out = refs[2 * n_parts : 2 * n_parts + 4]
    mt_ref, v_ref, u_ref, t_ref, r_ref, d_ref, v_sem, u_sem, out_sem = refs[2 * n_parts + 4 :]
    rows, cols = v_hbm.shape
    blocks = rows // 256
    order = [(g, p, at) for p, part in enumerate(parts) for at, g in enumerate(part)]
    v_copies, out_copies, u_copies = [], [], []
    for b in range(blocks):
        at = pl.ds(b * 256, 256)
        v_copies.append(pltpu.make_async_copy(v_hbm.at[at], v_ref.at[at], v_sem.at[b]))
        out_copies.append(pltpu.make_async_copy(r_ref.at[at], vectors_hbm.at[at], out_sem.at[b]))
    for n, (_, p, at) in enumerate(order):
        u_copies.append(
            [
                pltpu.make_async_copy(u_hbms[p].at[at], u_ref.at[n], u_sem.at[0, n]),
                pltpu.make_async_copy(t_hbms[p].at[at], t_ref.at[n], u_sem.at[1, n]),
            ]
        )
    early, late = range(len(order) // 2), range(len(order) // 2, len(order))
    for n in early:
        for c in u_copies[n]:
            c.start()
    for c in v_copies:
        c.start()
    for n in late:
        for c in u_copies[n]:
            c.start()
    mt_ref[...] = mix_ref[...].T
    mix = mt_ref[...]
    weight = weight_ref[...]
    down, along = iota((256, 256), 0), iota((256, 256), 1)
    same_atom = (down & (GROUP - 1)) == (along & (GROUP - 1))
    spread = ((down >> 4) == (along & (NPMAX - 1))).astype(jnp.float32).astype(jnp.bfloat16)
    same_i = (down >> 4) == (along >> 4)

    def rotate(b):
        at = slice(b * 256, (b + 1) * 256)
        panel = jnp.concatenate([own_ref[at, :], other_ref[at, :]], axis=1)
        turned = v_ref[at, :].astype(jnp.float32) - dot(panel, mix)
        r_ref[at, :] = turned.astype(jnp.bfloat16)

    def project(n):
        turned = u_ref[n].astype(jnp.float32) - dot(t_ref[n], mix)
        return turned.astype(jnp.bfloat16)

    def pair(rounded):
        weighted = (rounded.astype(jnp.float32) * weight).astype(jnp.bfloat16)
        return jnp.where(same_atom, dot(weighted, rounded, NT), 0.0)

    def pack(n, pairs):
        high = pairs.astype(jnp.bfloat16)
        low = (pairs - high.astype(jnp.float32)).astype(jnp.bfloat16)
        spreaded = jnp.where(same_i, dot(high, spread) + dot(low, spread), 0.0)
        total = spreaded[:GROUP]
        for i in range(1, NPMAX):
            total = total + spreaded[i * GROUP : (i + 1) * GROUP]
        at = order[n][0] * GROUP
        d_ref[at : at + GROUP, :] = total

    def densities(which):
        for n in which:
            for c in u_copies[n]:
                c.wait()
        projected, paired = {}, {}
        for n in range(which[0], which[-1] + 3):
            if n in which:
                projected[n] = project(n)
            if n - 1 in which:
                paired[n - 1] = pair(projected.pop(n - 1))
            if n - 2 in which:
                pack(n - 2, paired.pop(n - 2))

    densities(early)
    for c in v_copies:
        c.wait()
    for b in range(blocks):
        rotate(b)
    for c in out_copies:
        c.start()
    densities(late)
    per = own_out.shape[0]
    mine = pl.multiple_of(col_ref[0] * per, per)
    own_out[...] = d_ref[pl.ds(mine, per), :]
    other_out[...] = d_ref[pl.ds(per - mine, per), :]
    for c in out_copies:
        c.wait()


VMEM_SPEC = pl.BlockSpec(memory_space=VM)
SMEM_SPEC = pl.BlockSpec(memory_space=SM)
HBM_SPEC = pl.BlockSpec(memory_space=pltpu.MemorySpace.HBM)
BF16, F32 = jnp.bfloat16, jnp.float32


def in_hbm(x):
    return pltpu.with_memory_space_constraint(x, pltpu.MemorySpace.HBM)


def call(kernel, out_shape, in_specs, out_specs, flops, nbytes, mib, **kw):
    return pl.pallas_call(
        kernel,
        out_shape=out_shape,
        in_specs=in_specs,
        out_specs=out_specs,
        compiler_params=pltpu.CompilerParams(vmem_limit_bytes=mib * MIB),
        cost_estimate=pl.CostEstimate(flops=flops, bytes_accessed=nbytes, transcendentals=0),
        **kw,
    )


def partial_sums(panel, other, v_hbm):
    rows, cols = v_hbm.shape
    half = panel.shape[1]
    work = 2 * rows * cols * half
    done, v_vmem = call(
        own_kernel,
        [pltpu.VMEM((cols, half), BF16), pltpu.VMEM((rows, cols), BF16)],
        [HBM_SPEC, HBM_SPEC],
        [VMEM_SPEC, VMEM_SPEC],
        work,
        5 << 20,
        24,
        scratch_shapes=[
            pltpu.VMEM((rows, half), BF16),
            pltpu.VMEM((half, cols), F32),
            pltpu.SemaphoreType.DMA((rows // 256 + 1,)),
        ],
    )(in_hbm(panel), v_hbm)
    return call(
        other_kernel,
        pltpu.VMEM((cols, 2 * half), BF16),
        [VMEM_SPEC] * 3,
        VMEM_SPEC,
        work,
        5 << 20,
        24,
    )(done, other, v_vmem)


def couple(which, counts, present, proj_count, blocks, halos, v_hbm, panel, other):
    rows, cols = v_hbm.shape
    npan = 2 * panel.shape[1]
    atoms = counts.shape[0]
    n = len(which)

    first = not halos

    def kernel(counts_ref, present_ref, proj_ref, cm_ref, *rest):
        ends = (None, None) if first else rest[:2]
        rest = rest[len(halos) :]
        rim_refs = rest[6:8] if first else None
        rest = rest[:6] + rest[8:] if first else rest
        pre_kernel(which, rim_refs, counts_ref, present_ref, proj_ref, cm_ref, *ends, *rest)

    return call(
        kernel,
        [
            pltpu.HBM((n, 256, cols), BF16),
            pltpu.HBM((n, 256, npan), BF16),
            jax.ShapeDtypeStruct((1,), jnp.int32),
        ]
        + [jax.ShapeDtypeStruct((EDGE, cols + npan), BF16)] * (2 if first else 0),
        [SMEM_SPEC] + [VMEM_SPEC] * (3 + len(halos)) + [HBM_SPEC] * 3,
        [HBM_SPEC, HBM_SPEC, SMEM_SPEC] + [VMEM_SPEC] * (2 if first else 0),
        n * 2 * 256 * WIDE * (WIDE + cols + npan),
        10 << 20,
        28,
        scratch_shapes=[
            pltpu.SMEM((atoms + 2 * RIM,), jnp.int32),
            pltpu.VMEM((n, 256, WIDE), BF16),
            pltpu.VMEM((16, atoms), F32),
            pltpu.VMEM((atoms, 16), F32),
            pltpu.VMEM((rows + 2 * EDGE, cols), BF16),
            pltpu.VMEM((rows + 2 * EDGE, npan), BF16),
            pltpu.VMEM((n, 256, cols), BF16),
            pltpu.VMEM((n, 256, npan), BF16),
            pltpu.SemaphoreType.DMA((3,)),
            pltpu.SemaphoreType.DMA((2, n)),
        ],
    )(counts, present, proj_count, blocks, *halos, v_hbm, panel, other)


def mix(col, mark, slices, factor):
    return call(
        mix_kernel,
        pltpu.VMEM(slices.shape, BF16),
        [SMEM_SPEC, SMEM_SPEC, VMEM_SPEC, VMEM_SPEC],
        VMEM_SPEC,
        1 << 24,
        1 << 20,
        8,
    )(col, mark, slices, factor)


def finish(parts, col, mixing, weights, panel, other, us, ts, v_hbm):
    rows, cols = v_hbm.shape
    npan = 2 * panel.shape[1]
    groups = sum(len(p) for p in parts)
    atoms = groups * GROUP
    return call(
        functools.partial(main_kernel, parts),
        [
            jax.ShapeDtypeStruct((rows, cols), BF16),
            jax.ShapeDtypeStruct((atoms // 2, 256), F32),
            jax.ShapeDtypeStruct((atoms // 2, 256), F32),
        ],
        [SMEM_SPEC] + [VMEM_SPEC] * 4 + [HBM_SPEC] * (2 * len(parts) + 1),
        [HBM_SPEC, VMEM_SPEC, VMEM_SPEC],
        6 << 30,
        14 << 20,
        28,
        scratch_shapes=[
            pltpu.VMEM((npan, cols), BF16),
            pltpu.VMEM((rows, cols), BF16),
            pltpu.VMEM((groups, 256, cols), BF16),
            pltpu.VMEM((groups, 256, npan), BF16),
            pltpu.VMEM((rows, cols), BF16),
            pltpu.VMEM((atoms, 256), F32),
            pltpu.SemaphoreType.DMA((rows // 256,)),
            pltpu.SemaphoreType.DMA((2, groups)),
            pltpu.SemaphoreType.DMA((rows // 256,)),
        ],
    )(col, mixing, weights, panel, other, *us, *ts, v_hbm)


def local(
    vectors_in, panel, factor, atom_basis, proj_count, coupling, block_present, occ_mask, occ_weight
):
    cols = vectors_in.shape[1]
    npan = 2 * panel.shape[1]
    counts = atom_basis[0]
    groups = counts.shape[0] // GROUP
    n_row = lax.axis_size("row")
    n_col = lax.axis_size("col")
    col = lax.axis_index("col")[None]
    v_hbm = in_hbm(vectors_in)

    other = lax.ppermute(panel, "col", [(0, 1), (1, 0)])
    partial = partial_sums(panel, other, v_hbm)
    slices = lax.all_to_all(partial, "row", 0, 0, tiled=True)
    slices = slices.reshape(n_row, cols // n_row, npan)

    early = list(range(1, groups // 2))
    late = list(range(groups // 2, groups)) + [0]
    shared = (counts, block_present.T, proj_count[None, :], coupling.transpose(1, 0, 2))
    u_early, t_early, mark, to_next, to_last = couple(early, *shared, (), v_hbm, panel, other)
    up = [(i, (i + 1) % n_row) for i in range(n_row)]
    before = lax.ppermute(to_next, "row", up)
    copies = mix(col, mark, slices, factor)
    after = lax.ppermute(to_last, "row", [(j, i) for i, j in up])
    mixing = lax.all_to_all(copies.reshape(cols, npan), "row", 0, 0, tiled=True)
    u_late, t_late, _ = couple(late, *shared, (before, after), v_hbm, panel, other)

    weights = (occ_mask.astype(F32) * occ_weight / (cols * n_col))[None, :]
    us, ts = [in_hbm(u_early), in_hbm(u_late)], [in_hbm(t_early), in_hbm(t_late)]
    vectors, own_part, other_part = finish(
        (early, late), col, mixing, weights, panel, other, us, ts, v_hbm
    )
    density = own_part + lax.ppermute(other_part, "col", [(0, 1), (1, 0)])
    return vectors, density


def solution(mesh):
    placed = (
        P("row", "col"),
        P("row", "col"),
        P(),
        P("row", None),
        P("row"),
        P("row", None, None),
        P("row", None),
        P("col"),
        P("col"),
    )
    return jax.shard_map(
        local,
        mesh=mesh,
        in_specs=placed,
        out_specs=(P("row", "col"), P(("row", "col"), None)),
        check_vma=False,
    )
```

```python
import functools

import jax
import jax.numpy as jnp
from jax import lax
from jax.experimental import pallas as pl
from jax.experimental.pallas import tpu as pltpu
from jax.sharding import PartitionSpec as P

NPMAX = 16
BMAX = 24
K = 9
RIM = 4
EDGE = RIM * BMAX
TAIL = 128
GROUP = 16
SPAN = GROUP + 2 * RIM
WIDE = 640
ALIGN = 64
MIB = 1024 * 1024

VM = pltpu.MemorySpace.VMEM
SM = pltpu.MemorySpace.SMEM
NT = (((1,), (1,)), ((), ()))
NN = (((1,), (0,)), ((), ()))


def dot(a, b, dims=NN, **kw):
    return lax.dot_general(a, b, dims, preferred_element_type=jnp.float32, **kw)


def iota(shape, dim):
    return lax.broadcasted_iota(jnp.int32, shape, dim)


def padded_rows(counts_ref, first_atom, first_row, sources):
    slot = iota((EDGE, 1), 0)
    target = jnp.full((EDGE, 1), -1, jnp.int32)
    row = first_row
    for t in range(RIM):
        count = counts_ref[first_atom + t]
        u = slot - t * BMAX
        target = jnp.where((u >= 0) & (u < count), row + u, target)
        row = row + count
    pick = (iota((EDGE, TAIL), 1) == target).astype(jnp.float32).astype(jnp.bfloat16)
    return [dot(pick, source) for source in sources]


def fill_rims(odd_ref, counts_ref, e_ref, p_ref, to_pair, to_other):
    atoms = counts_ref.shape[0]
    cols = e_ref.shape[1]
    end = e_ref.shape[0] - EDGE
    tail = counts_ref[atoms - 1]
    for t in range(1, RIM):
        tail = tail + counts_ref[atoms - 1 - t]
    ends = []
    for atom, row, at in (
        (atoms - RIM, TAIL - tail, slice(end - TAIL, end)),
        (0, 0, slice(EDGE, EDGE + TAIL)),
    ):
        ends.append(padded_rows(counts_ref, atom, row, [e_ref[at, :], p_ref[at, :]]))
    odd = odd_ref[0] == 1
    for last, first, at in zip(*ends, (slice(0, cols), slice(cols, None))):
        to_pair[:, at] = jnp.where(odd, first, last).astype(jnp.bfloat16)
        to_other[:, at] = jnp.where(odd, last, first).astype(jnp.bfloat16)


def pre_kernel(
    which_groups,
    rim_refs,
    odd_ref,
    counts_ref,
    present_ref,
    proj_ref,
    cm_ref,
    pair_ref,
    other_ref,
    v_hbm,
    own_hbm,
    other_hbm,
    u_hbm,
    t_hbm,
    mark_ref,
    pos_ref,
    cp_ref,
    mask_ref,
    column_ref,
    e_ref,
    p_ref,
    u_ref,
    t_ref,
    sem,
    out_sem,
):
    atoms = counts_ref.shape[0]
    rows, cols = v_hbm.shape
    half = own_hbm.shape[1]
    inner = pl.ds(EDGE, rows)
    copies = [
        pltpu.make_async_copy(v_hbm, e_ref.at[inner], sem.at[0]),
        pltpu.make_async_copy(own_hbm, p_ref.at[inner, pl.ds(0, half)], sem.at[1]),
        pltpu.make_async_copy(other_hbm, p_ref.at[inner, pl.ds(half, half)], sem.at[2]),
    ]
    for c in copies:
        c.start()
    out_copies = []
    below, above = slice(0, EDGE), slice(EDGE + rows, None)
    if pair_ref is None:
        for at in (below, above):
            e_ref[at, :] = jnp.zeros((EDGE, cols), jnp.bfloat16)
            p_ref[at, :] = jnp.zeros((EDGE, 2 * half), jnp.bfloat16)
    else:
        for parity, places in ((0, (above, below)), (1, (below, above))):

            @pl.when(odd_ref[0] == parity)
            def _():
                for rim_ref, at in zip((pair_ref, other_ref), places):
                    e_ref[at, :] = rim_ref[:, :cols]
                    p_ref[at, :] = rim_ref[:, cols:]

    mark_ref[0] = counts_ref[0]

    for t in range(RIM):
        pos_ref[t] = t * BMAX
        pos_ref[RIM + atoms + t] = EDGE + rows + t * BMAX

    def add(t, at):
        pos_ref[RIM + t] = at
        return at + counts_ref[t]

    lax.fori_loop(0, atoms, add, jnp.int32(EDGE), unroll=8)
    mask_ref[...] = jnp.zeros(mask_ref.shape, jnp.float32)
    mask_ref[:K, :] = present_ref[...].astype(jnp.float32)
    mask_ref[K : K + 1, :] = proj_ref[...].astype(jnp.float32)
    column_ref[...] = mask_ref[...].T
    lanes = NPMAX * BMAX
    lane = iota((8, WIDE), 1)
    which = lane // BMAX
    slot = lane - which * BMAX
    sub = iota((GROUP, lanes), 1) // BMAX
    starts, bands = [], []

    def multiply(n):
        if n == 0:
            for c in copies:
                c.wait()
            if rim_refs is not None:
                fill_rims(odd_ref, counts_ref, e_ref, p_ref, *rim_refs)
        window = pl.ds(pl.multiple_of(starts[n], ALIGN), WIDE)
        u_ref[n] = dot(bands[n], e_ref[window, :]).astype(jnp.bfloat16)
        t_ref[n] = dot(bands[n], p_ref[window, :]).astype(jnp.bfloat16)
        out_copies.append(pltpu.make_async_copy(u_ref.at[n], u_hbm.at[n], out_sem.at[0, n]))
        out_copies.append(pltpu.make_async_copy(t_ref.at[n], t_hbm.at[n], out_sem.at[1, n]))
        for c in out_copies[-2:]:
            c.start()

    for n, g in enumerate(which_groups):
        mine = slice(g * GROUP, (g + 1) * GROUP)
        first = pos_ref[g * GROUP]
        start = jnp.minimum((first // ALIGN) * ALIGN, rows + 2 * EDGE - WIDE)
        target = jnp.full((8, WIDE), -1, jnp.int32)
        for t in range(SPAN):
            atom = g * GROUP + t - RIM
            count = counts_ref[atom] if 0 <= atom < atoms else BMAX
            at = pos_ref[atom + RIM] - start
            target = jnp.where((which == t) & (slot < count), at + slot, target)
        pick = (iota((WIDE, WIDE), 0) == target[:1]).astype(jnp.float32).astype(jnp.bfloat16)
        kept = column_ref[mine, K : K + 1] > sub.astype(jnp.float32)
        x = []
        for k in range(K):
            block = cm_ref[k, mine, :].astype(jnp.float32)
            x.append(jnp.where((column_ref[mine, k : k + 1] > 0.0) & kept, block, 0.0))
        x += [None] * (NPMAX - K)
        for bit in (1, 2, 4, 8):
            low = (sub & bit) == 0
            new = list(x)
            for p in range(NPMAX):
                q = p + bit
                if p & bit or (x[p] is None and x[q] is None):
                    continue
                a, b = x[p], x[q]
                zero = jnp.zeros((GROUP, lanes), jnp.float32)
                b_up = zero if b is None else pltpu.roll(b, bit * BMAX, 1)
                a_down = zero if a is None else pltpu.roll(a, lanes - bit * BMAX, 1)
                new[p] = jnp.where(low, zero if a is None else a, b_up)
                new[q] = jnp.where(low, a_down, zero if b is None else b)
            x = new
        pad = jnp.zeros((GROUP, WIDE - lanes), jnp.float32)
        for i in range(NPMAX):
            wide = jnp.concatenate([x[i], pad], axis=1)
            halves = [wide[:8], pltpu.roll(wide[8:], 8 * BMAX, 1)]
            for _ in range(2):
                halves = [pltpu.roll(h, 0, 1, stride=BMAX // 2, stride_axis=0) for h in halves]
            skew = jnp.concatenate(halves, axis=0)
            cp_ref[n, i * GROUP : (i + 1) * GROUP, :] = skew.astype(jnp.bfloat16)
        bands.append(dot(cp_ref[n], pick, NT).astype(jnp.bfloat16))
        starts.append(start)
        multiply(n)
    for c in out_copies:
        c.wait()


def own_kernel(own_hbm, v_hbm, done_ref, v_ref, own_ref, acc_ref, sem):
    rows = v_hbm.shape[0]
    blocks = rows // 256
    at = [pl.ds(b * 256, 256) for b in range(blocks)]
    copies = [pltpu.make_async_copy(own_hbm, own_ref, sem.at[blocks])]
    copies += [pltpu.make_async_copy(v_hbm.at[s], v_ref.at[s], sem.at[b]) for b, s in enumerate(at)]
    for c in copies:
        c.start()
    copies[0].wait()
    turned = own_ref[...].T
    for b in range(blocks):
        copies[1 + b].wait()
        mine = slice(b * 256, (b + 1) * 256)
        product = dot(turned[:, mine], v_ref[mine, :])
        acc_ref[...] = product if b == 0 else acc_ref[...] + product
    done_ref[...] = acc_ref[...].T.astype(jnp.bfloat16)


def other_kernel(done_ref, other_ref, v_ref, out_hbm, out_ref, sem):
    half = other_ref.shape[1]
    cols = v_ref.shape[1]
    turned = other_ref[...].T
    copies = []
    for n, at in enumerate(range(0, cols, 256)):
        mine = slice(at, at + 256)
        out_ref[mine, :half] = done_ref[mine, :]
        out_ref[mine, half:] = dot(turned, v_ref[:, mine]).T.astype(jnp.bfloat16)
        piece = pl.ds(at, 256)
        copies.append(pltpu.make_async_copy(out_ref.at[piece], out_hbm.at[piece], sem.at[n]))
        copies[-1].start()
    for c in copies:
        c.wait()


def mix_kernel(col_ref, mark_ref, parts_ref, factor_ref, out_ref):
    total = jnp.sum(parts_ref[...].astype(jnp.float32), axis=0)
    half = total.shape[1] // 2
    swap = col_ref[0] == 1
    total = jnp.where(swap, pltpu.roll(total, half, 1), total)
    mixed = dot(total, factor_ref[...], precision=lax.Precision.HIGHEST)
    mixed = jnp.where(swap, pltpu.roll(mixed, half, 1), mixed).astype(jnp.bfloat16)
    out_ref[...] = jnp.broadcast_to(mixed[None], out_ref.shape)


def main_kernel(parts, col_ref, mix_ref, weight_ref, own_ref, other_ref, *refs):
    n_parts = len(parts)
    u_hbms, t_hbms = refs[:n_parts], refs[n_parts : 2 * n_parts]
    v_hbm, vectors_hbm, own_out, other_out = refs[2 * n_parts : 2 * n_parts + 4]
    mt_ref, v_ref, u_ref, t_ref, r_ref, d_ref, v_sem, u_sem, out_sem = refs[2 * n_parts + 4 :]
    rows, cols = v_hbm.shape
    blocks = rows // 256
    order = [(g, p, at) for p, part in enumerate(parts) for at, g in enumerate(part)]
    v_copies, out_copies, u_copies = [], [], []
    for b in range(blocks):
        at = pl.ds(b * 256, 256)
        v_copies.append(pltpu.make_async_copy(v_hbm.at[at], v_ref.at[at], v_sem.at[b]))
        out_copies.append(pltpu.make_async_copy(r_ref.at[at], vectors_hbm.at[at], out_sem.at[b]))
    for n, (_, p, at) in enumerate(order):
        u_copies.append(
            [
                pltpu.make_async_copy(u_hbms[p].at[at], u_ref.at[n], u_sem.at[0, n]),
                pltpu.make_async_copy(t_hbms[p].at[at], t_ref.at[n], u_sem.at[1, n]),
            ]
        )
    early, late = range(len(order) // 2), range(len(order) // 2, len(order))
    for n in early:
        for c in u_copies[n]:
            c.start()
    for c in v_copies:
        c.start()
    for n in late:
        for c in u_copies[n]:
            c.start()
    mt_ref[...] = mix_ref[...].T
    mix = mt_ref[...]
    weight = weight_ref[...]
    down, along = iota((256, 256), 0), iota((256, 256), 1)
    same_atom = (down & (GROUP - 1)) == (along & (GROUP - 1))
    spread = ((down >> 4) == (along & (NPMAX - 1))).astype(jnp.float32).astype(jnp.bfloat16)
    same_i = (down >> 4) == (along >> 4)

    def rotate(b):
        at = slice(b * 256, (b + 1) * 256)
        panel = jnp.concatenate([own_ref[at, :], other_ref[at, :]], axis=1)
        turned = v_ref[at, :].astype(jnp.float32) - dot(panel, mix)
        r_ref[at, :] = turned.astype(jnp.bfloat16)

    def project(n):
        turned = u_ref[n].astype(jnp.float32) - dot(t_ref[n], mix)
        return turned.astype(jnp.bfloat16)

    def pair(rounded):
        weighted = (rounded.astype(jnp.float32) * weight).astype(jnp.bfloat16)
        return jnp.where(same_atom, dot(weighted, rounded, NT), 0.0)

    def pack(n, pairs):
        high = pairs.astype(jnp.bfloat16)
        low = (pairs - high.astype(jnp.float32)).astype(jnp.bfloat16)
        spreaded = jnp.where(same_i, dot(high, spread) + dot(low, spread), 0.0)
        total = spreaded[:GROUP]
        for i in range(1, NPMAX):
            total = total + spreaded[i * GROUP : (i + 1) * GROUP]
        at = order[n][0] * GROUP
        d_ref[at : at + GROUP, :] = total

    def densities(which):
        for n in which:
            for c in u_copies[n]:
                c.wait()
        projected, paired = {}, {}
        for n in range(which[0], which[-1] + 3):
            if n in which:
                projected[n] = project(n)
            if n - 1 in which:
                paired[n - 1] = pair(projected.pop(n - 1))
            if n - 2 in which:
                pack(n - 2, paired.pop(n - 2))

    densities(early)
    for c in v_copies:
        c.wait()
    for b in range(blocks):
        rotate(b)
    for c in out_copies:
        c.start()
    densities(late)
    per = own_out.shape[0]
    mine = pl.multiple_of(col_ref[0] * per, per)
    own_out[...] = d_ref[pl.ds(mine, per), :]
    other_out[...] = d_ref[pl.ds(per - mine, per), :]
    for c in out_copies:
        c.wait()


VMEM_SPEC = pl.BlockSpec(memory_space=VM)
SMEM_SPEC = pl.BlockSpec(memory_space=SM)
HBM_SPEC = pl.BlockSpec(memory_space=pltpu.MemorySpace.HBM)
BF16, F32 = jnp.bfloat16, jnp.float32


def in_hbm(x):
    return pltpu.with_memory_space_constraint(x, pltpu.MemorySpace.HBM)


def call(kernel, out_shape, in_specs, out_specs, flops, nbytes, mib, **kw):
    return pl.pallas_call(
        kernel,
        out_shape=out_shape,
        in_specs=in_specs,
        out_specs=out_specs,
        compiler_params=pltpu.CompilerParams(vmem_limit_bytes=mib * MIB),
        cost_estimate=pl.CostEstimate(flops=flops, bytes_accessed=nbytes, transcendentals=0),
        **kw,
    )


def partial_sums(panel, other, v_hbm):
    rows, cols = v_hbm.shape
    half = panel.shape[1]
    work = 2 * rows * cols * half
    done, v_vmem = call(
        own_kernel,
        [pltpu.VMEM((cols, half), BF16), pltpu.VMEM((rows, cols), BF16)],
        [HBM_SPEC, HBM_SPEC],
        [VMEM_SPEC, VMEM_SPEC],
        work,
        5 << 20,
        24,
        scratch_shapes=[
            pltpu.VMEM((rows, half), BF16),
            pltpu.VMEM((half, cols), F32),
            pltpu.SemaphoreType.DMA((rows // 256 + 1,)),
        ],
    )(in_hbm(panel), v_hbm)
    return call(
        other_kernel,
        pltpu.HBM((cols, 2 * half), BF16),
        [VMEM_SPEC] * 3,
        HBM_SPEC,
        work,
        5 << 20,
        24,
        scratch_shapes=[
            pltpu.VMEM((cols, 2 * half), BF16),
            pltpu.SemaphoreType.DMA((cols // 256,)),
        ],
    )(done, other, v_vmem)


def couple(which, odd, counts, present, proj_count, blocks, halos, v_hbm, panel, other):
    rows, cols = v_hbm.shape
    npan = 2 * panel.shape[1]
    atoms = counts.shape[0]
    n = len(which)

    first = not halos

    def kernel(odd_ref, counts_ref, present_ref, proj_ref, cm_ref, *rest):
        ends = (None, None) if first else rest[:2]
        rest = rest[len(halos) :]
        rim_refs = rest[6:8] if first else None
        rest = rest[:6] + rest[8:] if first else rest
        shared = (odd_ref, counts_ref, present_ref, proj_ref, cm_ref)
        pre_kernel(which, rim_refs, *shared, *ends, *rest)

    return call(
        kernel,
        [
            pltpu.HBM((n, 256, cols), BF16),
            pltpu.HBM((n, 256, npan), BF16),
            jax.ShapeDtypeStruct((1,), jnp.int32),
        ]
        + [jax.ShapeDtypeStruct((EDGE, cols + npan), BF16)] * (2 if first else 0),
        [SMEM_SPEC] * 2 + [VMEM_SPEC] * (3 + len(halos)) + [HBM_SPEC] * 3,
        [HBM_SPEC, HBM_SPEC, SMEM_SPEC] + [VMEM_SPEC] * (2 if first else 0),
        n * 2 * 256 * WIDE * (WIDE + cols + npan),
        10 << 20,
        28,
        scratch_shapes=[
            pltpu.SMEM((atoms + 2 * RIM,), jnp.int32),
            pltpu.VMEM((n, 256, WIDE), BF16),
            pltpu.VMEM((16, atoms), F32),
            pltpu.VMEM((atoms, 16), F32),
            pltpu.VMEM((rows + 2 * EDGE, cols), BF16),
            pltpu.VMEM((rows + 2 * EDGE, npan), BF16),
            pltpu.VMEM((n, 256, cols), BF16),
            pltpu.VMEM((n, 256, npan), BF16),
            pltpu.SemaphoreType.DMA((3,)),
            pltpu.SemaphoreType.DMA((2, n)),
        ],
    )(odd, counts, present, proj_count, blocks, *halos, v_hbm, panel, other)


def mix(col, mark, slices, factor):
    return call(
        mix_kernel,
        pltpu.VMEM(slices.shape, BF16),
        [SMEM_SPEC, SMEM_SPEC, VMEM_SPEC, VMEM_SPEC],
        VMEM_SPEC,
        1 << 24,
        1 << 20,
        8,
    )(col, mark, slices, factor)


def finish(parts, col, mixing, weights, panel, other, us, ts, v_hbm):
    rows, cols = v_hbm.shape
    npan = 2 * panel.shape[1]
    groups = sum(len(p) for p in parts)
    atoms = groups * GROUP
    return call(
        functools.partial(main_kernel, parts),
        [
            jax.ShapeDtypeStruct((rows, cols), BF16),
            jax.ShapeDtypeStruct((atoms // 2, 256), F32),
            jax.ShapeDtypeStruct((atoms // 2, 256), F32),
        ],
        [SMEM_SPEC] + [VMEM_SPEC] * 4 + [HBM_SPEC] * (2 * len(parts) + 1),
        [HBM_SPEC, VMEM_SPEC, VMEM_SPEC],
        6 << 30,
        14 << 20,
        28,
        scratch_shapes=[
            pltpu.VMEM((npan, cols), BF16),
            pltpu.VMEM((rows, cols), BF16),
            pltpu.VMEM((groups, 256, cols), BF16),
            pltpu.VMEM((groups, 256, npan), BF16),
            pltpu.VMEM((rows, cols), BF16),
            pltpu.VMEM((atoms, 256), F32),
            pltpu.SemaphoreType.DMA((rows // 256,)),
            pltpu.SemaphoreType.DMA((2, groups)),
            pltpu.SemaphoreType.DMA((rows // 256,)),
        ],
    )(col, mixing, weights, panel, other, *us, *ts, v_hbm)


def local(
    vectors_in, panel, factor, atom_basis, proj_count, coupling, block_present, occ_mask, occ_weight
):
    cols = vectors_in.shape[1]
    npan = 2 * panel.shape[1]
    counts = atom_basis[0]
    groups = counts.shape[0] // GROUP
    n_row = lax.axis_size("row")
    n_col = lax.axis_size("col")
    col = lax.axis_index("col")[None]
    v_hbm = in_hbm(vectors_in)

    other = lax.ppermute(panel, "col", [(0, 1), (1, 0)])
    partial = partial_sums(panel, other, v_hbm)
    slices = lax.all_to_all(partial, "row", 0, 0, tiled=True)
    slices = slices.reshape(n_row, cols // n_row, npan)

    early = list(range(1, groups // 2))
    late = list(range(groups // 2, groups)) + [0]
    odd = (lax.axis_index("row") & 1)[None]
    shared = (odd, counts, block_present.T, proj_count[None, :], coupling.transpose(1, 0, 2))
    u_early, t_early, mark, to_pair, to_other = couple(early, *shared, (), v_hbm, panel, other)
    firsts = range(0, n_row, 2)
    pairs = [(i, i + 1) for i in firsts]
    others = [(i + 1, (i + 2) % n_row) for i in firsts]
    rim_pair = lax.ppermute(to_pair, "row", pairs + [(j, i) for i, j in pairs])
    rim_other = lax.ppermute(to_other, "row", others + [(j, i) for i, j in others])
    copies = mix(col, mark, slices, factor)
    mixing = lax.all_to_all(copies.reshape(cols, npan), "row", 0, 0, tiled=True)
    u_late, t_late, _ = couple(late, *shared, (rim_pair, rim_other), v_hbm, panel, other)

    weights = (occ_mask.astype(F32) * occ_weight / (cols * n_col))[None, :]
    us, ts = [in_hbm(u_early), in_hbm(u_late)], [in_hbm(t_early), in_hbm(t_late)]
    vectors, own_part, other_part = finish(
        (early, late), col, mixing, weights, panel, other, us, ts, v_hbm
    )
    density = own_part + lax.ppermute(other_part, "col", [(0, 1), (1, 0)])
    return vectors, density


def solution(mesh):
    placed = (
        P("row", "col"),
        P("row", "col"),
        P(),
        P("row", None),
        P("row"),
        P("row", None, None),
        P("row", None),
        P("col"),
        P("col"),
    )
    return jax.shard_map(
        local,
        mesh=mesh,
        in_specs=placed,
        out_specs=(P("row", "col"), P(("row", "col"), None)),
        check_vma=False,
    )
```

```python
import functools

import jax
import jax.numpy as jnp
from jax import lax
from jax.experimental import pallas as pl
from jax.experimental.pallas import tpu as pltpu
from jax.sharding import PartitionSpec as P

NPMAX = 16
BMAX = 24
K = 9
RIM = 4
EDGE = RIM * BMAX
TAIL = 128
GROUP = 16
SPAN = GROUP + 2 * RIM
WIDE = 640
ALIGN = 64
MIB = 1024 * 1024

VM = pltpu.MemorySpace.VMEM
SM = pltpu.MemorySpace.SMEM
NT = (((1,), (1,)), ((), ()))
NN = (((1,), (0,)), ((), ()))


def dot(a, b, dims=NN, **kw):
    return lax.dot_general(a, b, dims, preferred_element_type=jnp.float32, **kw)


def iota(shape, dim):
    return lax.broadcasted_iota(jnp.int32, shape, dim)


def padded_rows(counts_ref, first_atom, first_row, sources):
    slot = iota((EDGE, 1), 0)
    target = jnp.full((EDGE, 1), -1, jnp.int32)
    row = first_row
    for t in range(RIM):
        count = counts_ref[first_atom + t]
        u = slot - t * BMAX
        target = jnp.where((u >= 0) & (u < count), row + u, target)
        row = row + count
    pick = (iota((EDGE, TAIL), 1) == target).astype(jnp.float32).astype(jnp.bfloat16)
    return [dot(pick, source).astype(jnp.bfloat16) for source in sources]


def fill_rims(counts_ref, e_ref, p_ref, to_next, to_last):
    atoms = counts_ref.shape[0]
    cols = e_ref.shape[1]
    end = e_ref.shape[0] - EDGE
    tail = counts_ref[atoms - 1]
    for t in range(1, RIM):
        tail = tail + counts_ref[atoms - 1 - t]
    for out, atom, row, at in (
        (to_next, atoms - RIM, TAIL - tail, slice(end - TAIL, end)),
        (to_last, 0, 0, slice(EDGE, EDGE + TAIL)),
    ):
        pieces = padded_rows(counts_ref, atom, row, [e_ref[at, :], p_ref[at, :]])
        out[:, :cols] = pieces[0]
        out[:, cols:] = pieces[1]


def pre_kernel(
    which_groups,
    rim_refs,
    counts_ref,
    present_ref,
    proj_ref,
    cm_ref,
    before_ref,
    after_ref,
    v_hbm,
    own_hbm,
    other_hbm,
    u_hbm,
    t_hbm,
    mark_ref,
    pos_ref,
    cp_ref,
    mask_ref,
    column_ref,
    e_ref,
    p_ref,
    u_ref,
    t_ref,
    sem,
    out_sem,
):
    atoms = counts_ref.shape[0]
    rows, cols = v_hbm.shape
    half = own_hbm.shape[1]
    inner = pl.ds(EDGE, rows)
    copies = [
        pltpu.make_async_copy(v_hbm, e_ref.at[inner], sem.at[0]),
        pltpu.make_async_copy(own_hbm, p_ref.at[inner, pl.ds(0, half)], sem.at[1]),
        pltpu.make_async_copy(other_hbm, p_ref.at[inner, pl.ds(half, half)], sem.at[2]),
    ]
    for c in copies:
        c.start()
    out_copies = []
    for halo_ref, at in ((before_ref, 0), (after_ref, EDGE + rows)):
        mine = slice(at, at + EDGE)
        if halo_ref is None:
            e_ref[mine, :] = jnp.zeros((EDGE, cols), jnp.bfloat16)
            p_ref[mine, :] = jnp.zeros((EDGE, 2 * half), jnp.bfloat16)
        else:
            e_ref[mine, :] = halo_ref[:, :cols]
            p_ref[mine, :] = halo_ref[:, cols:]
    mark_ref[0] = counts_ref[0]

    for t in range(RIM):
        pos_ref[t] = t * BMAX
        pos_ref[RIM + atoms + t] = EDGE + rows + t * BMAX

    def add(t, at):
        pos_ref[RIM + t] = at
        return at + counts_ref[t]

    lax.fori_loop(0, atoms, add, jnp.int32(EDGE), unroll=8)
    mask_ref[...] = jnp.zeros(mask_ref.shape, jnp.float32)
    mask_ref[:K, :] = present_ref[...].astype(jnp.float32)
    mask_ref[K : K + 1, :] = proj_ref[...].astype(jnp.float32)
    column_ref[...] = mask_ref[...].T
    lanes = NPMAX * BMAX
    lane = iota((8, WIDE), 1)
    which = lane // BMAX
    slot = lane - which * BMAX
    sub = iota((GROUP, lanes), 1) // BMAX
    starts, bands = [], []

    def multiply(n):
        if n == 0:
            for c in copies:
                c.wait()
            if rim_refs is not None:
                fill_rims(counts_ref, e_ref, p_ref, *rim_refs)
        window = pl.ds(pl.multiple_of(starts[n], ALIGN), WIDE)
        u_ref[n] = dot(bands[n], e_ref[window, :]).astype(jnp.bfloat16)
        t_ref[n] = dot(bands[n], p_ref[window, :]).astype(jnp.bfloat16)
        out_copies.append(pltpu.make_async_copy(u_ref.at[n], u_hbm.at[n], out_sem.at[0, n]))
        out_copies.append(pltpu.make_async_copy(t_ref.at[n], t_hbm.at[n], out_sem.at[1, n]))
        for c in out_copies[-2:]:
            c.start()

    for n, g in enumerate(which_groups):
        mine = slice(g * GROUP, (g + 1) * GROUP)
        first = pos_ref[g * GROUP]
        start = jnp.minimum((first // ALIGN) * ALIGN, rows + 2 * EDGE - WIDE)
        target = jnp.full((8, WIDE), -1, jnp.int32)
        for t in range(SPAN):
            atom = g * GROUP + t - RIM
            count = counts_ref[atom] if 0 <= atom < atoms else BMAX
            at = pos_ref[atom + RIM] - start
            target = jnp.where((which == t) & (slot < count), at + slot, target)
        pick = (iota((WIDE, WIDE), 0) == target[:1]).astype(jnp.float32).astype(jnp.bfloat16)
        kept = column_ref[mine, K : K + 1] > sub.astype(jnp.float32)
        x = []
        for k in range(K):
            block = cm_ref[k, mine, :].astype(jnp.float32)
            x.append(jnp.where((column_ref[mine, k : k + 1] > 0.0) & kept, block, 0.0))
        x += [None] * (NPMAX - K)
        for bit in (1, 2, 4, 8):
            low = (sub & bit) == 0
            new = list(x)
            for p in range(NPMAX):
                q = p + bit
                if p & bit or (x[p] is None and x[q] is None):
                    continue
                a, b = x[p], x[q]
                zero = jnp.zeros((GROUP, lanes), jnp.float32)
                b_up = zero if b is None else pltpu.roll(b, bit * BMAX, 1)
                a_down = zero if a is None else pltpu.roll(a, lanes - bit * BMAX, 1)
                new[p] = jnp.where(low, zero if a is None else a, b_up)
                new[q] = jnp.where(low, a_down, zero if b is None else b)
            x = new
        pad = jnp.zeros((GROUP, WIDE - lanes), jnp.float32)
        for i in range(NPMAX):
            wide = jnp.concatenate([x[i], pad], axis=1)
            halves = [wide[:8], pltpu.roll(wide[8:], 8 * BMAX, 1)]
            for _ in range(2):
                halves = [pltpu.roll(h, 0, 1, stride=BMAX // 2, stride_axis=0) for h in halves]
            skew = jnp.concatenate(halves, axis=0)
            cp_ref[n, i * GROUP : (i + 1) * GROUP, :] = skew.astype(jnp.bfloat16)
        bands.append(dot(cp_ref[n], pick, NT).astype(jnp.bfloat16))
        starts.append(start)
        multiply(n)
    for c in out_copies:
        c.wait()


def own_kernel(own_hbm, v_hbm, done_ref, v_ref, own_ref, acc_ref, sem):
    rows = v_hbm.shape[0]
    blocks = rows // 256
    at = [pl.ds(b * 256, 256) for b in range(blocks)]
    copies = [pltpu.make_async_copy(own_hbm, own_ref, sem.at[blocks])]
    copies += [pltpu.make_async_copy(v_hbm.at[s], v_ref.at[s], sem.at[b]) for b, s in enumerate(at)]
    for c in copies:
        c.start()
    copies[0].wait()
    turned = own_ref[...].T
    for b in range(blocks):
        copies[1 + b].wait()
        mine = slice(b * 256, (b + 1) * 256)
        product = dot(turned[:, mine], v_ref[mine, :])
        acc_ref[...] = product if b == 0 else acc_ref[...] + product
    done_ref[...] = acc_ref[...].T.astype(jnp.bfloat16)


def other_kernel(done_ref, other_ref, v_ref, out_ref):
    half = other_ref.shape[1]
    cols = v_ref.shape[1]
    turned = other_ref[...].T
    out_ref[:, :half] = done_ref[...]
    for at in range(0, cols, 256):
        mine = slice(at, at + 256)
        out_ref[mine, half:] = dot(turned, v_ref[:, mine]).T.astype(jnp.bfloat16)


def mix_kernel(col_ref, mark_ref, parts_ref, factor_ref, out_ref):
    total = jnp.sum(parts_ref[...].astype(jnp.float32), axis=0)
    half = total.shape[1] // 2
    swap = col_ref[0] == 1
    total = jnp.where(swap, pltpu.roll(total, half, 1), total)
    mixed = dot(total, factor_ref[...], precision=lax.Precision.HIGHEST)
    mixed = jnp.where(swap, pltpu.roll(mixed, half, 1), mixed).astype(jnp.bfloat16)
    out_ref[...] = jnp.broadcast_to(mixed[None], out_ref.shape)


def main_kernel(parts, col_ref, mix_ref, weight_ref, own_ref, other_ref, *refs):
    n_parts = len(parts)
    u_hbms, t_hbms = refs[:n_parts], refs[n_parts : 2 * n_parts]
    v_hbm, vectors_hbm, own_out, other_out = refs[2 * n_parts : 2 * n_parts + 4]
    mt_ref, v_ref, u_ref, t_ref, r_ref, d_ref, v_sem, u_sem, out_sem = refs[2 * n_parts + 4 :]
    rows, cols = v_hbm.shape
    blocks = rows // 256
    order = [(g, p, at) for p, part in enumerate(parts) for at, g in enumerate(part)]
    v_copies, out_copies, u_copies = [], [], []
    for b in range(blocks):
        at = pl.ds(b * 256, 256)
        v_copies.append(pltpu.make_async_copy(v_hbm.at[at], v_ref.at[at], v_sem.at[b]))
        out_copies.append(pltpu.make_async_copy(r_ref.at[at], vectors_hbm.at[at], out_sem.at[b]))
    for n, (_, p, at) in enumerate(order):
        u_copies.append(
            [
                pltpu.make_async_copy(u_hbms[p].at[at], u_ref.at[n], u_sem.at[0, n]),
                pltpu.make_async_copy(t_hbms[p].at[at], t_ref.at[n], u_sem.at[1, n]),
            ]
        )
    early, late = range(len(order) // 2), range(len(order) // 2, len(order))
    for n in early:
        for c in u_copies[n]:
            c.start()
    for c in v_copies:
        c.start()
    for n in late:
        for c in u_copies[n]:
            c.start()
    mt_ref[...] = mix_ref[...].T
    mix = mt_ref[...]
    weight = weight_ref[...]
    down, along = iota((256, 256), 0), iota((256, 256), 1)
    same_atom = (down & (GROUP - 1)) == (along & (GROUP - 1))
    spread = ((down >> 4) == (along & (NPMAX - 1))).astype(jnp.float32).astype(jnp.bfloat16)
    same_i = (down >> 4) == (along >> 4)

    def rotate(b):
        at = slice(b * 256, (b + 1) * 256)
        panel = jnp.concatenate([own_ref[at, :], other_ref[at, :]], axis=1)
        turned = v_ref[at, :].astype(jnp.float32) - dot(panel, mix)
        r_ref[at, :] = turned.astype(jnp.bfloat16)

    def project(n):
        turned = u_ref[n].astype(jnp.float32) - dot(t_ref[n], mix)
        return turned.astype(jnp.bfloat16)

    def pair(rounded):
        weighted = (rounded.astype(jnp.float32) * weight).astype(jnp.bfloat16)
        return jnp.where(same_atom, dot(weighted, rounded, NT), 0.0)

    def pack(n, pairs):
        high = pairs.astype(jnp.bfloat16)
        low = (pairs - high.astype(jnp.float32)).astype(jnp.bfloat16)
        spreaded = jnp.where(same_i, dot(high, spread) + dot(low, spread), 0.0)
        total = spreaded[:GROUP]
        for i in range(1, NPMAX):
            total = total + spreaded[i * GROUP : (i + 1) * GROUP]
        at = order[n][0] * GROUP
        d_ref[at : at + GROUP, :] = total

    def densities(which):
        for n in which:
            for c in u_copies[n]:
                c.wait()
        projected, paired = {}, {}
        for n in range(which[0], which[-1] + 3):
            if n in which:
                projected[n] = project(n)
            if n - 1 in which:
                paired[n - 1] = pair(projected.pop(n - 1))
            if n - 2 in which:
                pack(n - 2, paired.pop(n - 2))

    densities(early)
    for c in v_copies:
        c.wait()
    for b in range(blocks):
        rotate(b)
    for c in out_copies:
        c.start()
    densities(late)
    per = own_out.shape[0]
    mine = pl.multiple_of(col_ref[0] * per, per)
    own_out[...] = d_ref[pl.ds(mine, per), :]
    other_out[...] = d_ref[pl.ds(per - mine, per), :]
    for c in out_copies:
        c.wait()


VMEM_SPEC = pl.BlockSpec(memory_space=VM)
SMEM_SPEC = pl.BlockSpec(memory_space=SM)
HBM_SPEC = pl.BlockSpec(memory_space=pltpu.MemorySpace.HBM)
BF16, F32 = jnp.bfloat16, jnp.float32


def in_hbm(x):
    return pltpu.with_memory_space_constraint(x, pltpu.MemorySpace.HBM)


def call(kernel, out_shape, in_specs, out_specs, flops, nbytes, mib, **kw):
    return pl.pallas_call(
        kernel,
        out_shape=out_shape,
        in_specs=in_specs,
        out_specs=out_specs,
        compiler_params=pltpu.CompilerParams(vmem_limit_bytes=mib * MIB),
        cost_estimate=pl.CostEstimate(flops=flops, bytes_accessed=nbytes, transcendentals=0),
        **kw,
    )


def partial_sums(panel, other, v_hbm):
    rows, cols = v_hbm.shape
    half = panel.shape[1]
    work = 2 * rows * cols * half
    done, v_vmem = call(
        own_kernel,
        [pltpu.VMEM((cols, half), BF16), pltpu.VMEM((rows, cols), BF16)],
        [HBM_SPEC, HBM_SPEC],
        [VMEM_SPEC, VMEM_SPEC],
        work,
        5 << 20,
        24,
        scratch_shapes=[
            pltpu.VMEM((rows, half), BF16),
            pltpu.VMEM((half, cols), F32),
            pltpu.SemaphoreType.DMA((rows // 256 + 1,)),
        ],
    )(in_hbm(panel), v_hbm)
    return call(
        other_kernel,
        pltpu.VMEM((cols, 2 * half), BF16),
        [VMEM_SPEC] * 3,
        VMEM_SPEC,
        work,
        5 << 20,
        24,
    )(done, other, v_vmem)


def couple(which, counts, present, proj_count, blocks, halos, v_hbm, panel, other):
    rows, cols = v_hbm.shape
    npan = 2 * panel.shape[1]
    atoms = counts.shape[0]
    n = len(which)

    first = not halos

    def kernel(counts_ref, present_ref, proj_ref, cm_ref, *rest):
        ends = (None, None) if first else rest[:2]
        rest = rest[len(halos) :]
        rim_refs = rest[6:8] if first else None
        rest = rest[:6] + rest[8:] if first else rest
        pre_kernel(which, rim_refs, counts_ref, present_ref, proj_ref, cm_ref, *ends, *rest)

    return call(
        kernel,
        [
            pltpu.HBM((n, 256, cols), BF16),
            pltpu.HBM((n, 256, npan), BF16),
            jax.ShapeDtypeStruct((1,), jnp.int32),
        ]
        + [jax.ShapeDtypeStruct((EDGE, cols + npan), BF16)] * (2 if first else 0),
        [SMEM_SPEC] + [VMEM_SPEC] * (3 + len(halos)) + [HBM_SPEC] * 3,
        [HBM_SPEC, HBM_SPEC, SMEM_SPEC] + [VMEM_SPEC] * (2 if first else 0),
        n * 2 * 256 * WIDE * (WIDE + cols + npan),
        10 << 20,
        28,
        scratch_shapes=[
            pltpu.SMEM((atoms + 2 * RIM,), jnp.int32),
            pltpu.VMEM((n, 256, WIDE), BF16),
            pltpu.VMEM((16, atoms), F32),
            pltpu.VMEM((atoms, 16), F32),
            pltpu.VMEM((rows + 2 * EDGE, cols), BF16),
            pltpu.VMEM((rows + 2 * EDGE, npan), BF16),
            pltpu.VMEM((n, 256, cols), BF16),
            pltpu.VMEM((n, 256, npan), BF16),
            pltpu.SemaphoreType.DMA((3,)),
            pltpu.SemaphoreType.DMA((2, n)),
        ],
    )(counts, present, proj_count, blocks, *halos, v_hbm, panel, other)


def mix(col, mark, slices, factor):
    return call(
        mix_kernel,
        pltpu.VMEM(slices.shape, BF16),
        [SMEM_SPEC, SMEM_SPEC, VMEM_SPEC, VMEM_SPEC],
        VMEM_SPEC,
        1 << 24,
        1 << 20,
        8,
    )(col, mark, slices, factor)


def finish(parts, col, mixing, weights, panel, other, us, ts, v_hbm):
    rows, cols = v_hbm.shape
    npan = 2 * panel.shape[1]
    groups = sum(len(p) for p in parts)
    atoms = groups * GROUP
    return call(
        functools.partial(main_kernel, parts),
        [
            jax.ShapeDtypeStruct((rows, cols), BF16),
            jax.ShapeDtypeStruct((atoms // 2, 256), F32),
            jax.ShapeDtypeStruct((atoms // 2, 256), F32),
        ],
        [SMEM_SPEC] + [VMEM_SPEC] * 4 + [HBM_SPEC] * (2 * len(parts) + 1),
        [HBM_SPEC, VMEM_SPEC, VMEM_SPEC],
        6 << 30,
        14 << 20,
        28,
        scratch_shapes=[
            pltpu.VMEM((npan, cols), BF16),
            pltpu.VMEM((rows, cols), BF16),
            pltpu.VMEM((groups, 256, cols), BF16),
            pltpu.VMEM((groups, 256, npan), BF16),
            pltpu.VMEM((rows, cols), BF16),
            pltpu.VMEM((atoms, 256), F32),
            pltpu.SemaphoreType.DMA((rows // 256,)),
            pltpu.SemaphoreType.DMA((2, groups)),
            pltpu.SemaphoreType.DMA((rows // 256,)),
        ],
    )(col, mixing, weights, panel, other, *us, *ts, v_hbm)


def local(
    vectors_in, panel, factor, atom_basis, proj_count, coupling, block_present, occ_mask, occ_weight
):
    cols = vectors_in.shape[1]
    npan = 2 * panel.shape[1]
    counts = atom_basis[0]
    groups = counts.shape[0] // GROUP
    n_row = lax.axis_size("row")
    n_col = lax.axis_size("col")
    col = lax.axis_index("col")[None]
    v_hbm = in_hbm(vectors_in)

    other = lax.ppermute(panel, "col", [(0, 1), (1, 0)])
    partial = partial_sums(panel, other, v_hbm)
    forward = [i * n_col for i in range(n_row)]
    groups_of = [forward] + [[i + c for i in reversed(forward)] for c in range(1, n_col)]
    exchange = functools.partial(
        lax.all_to_all,
        axis_name=("row", "col"),
        split_axis=0,
        concat_axis=0,
        axis_index_groups=groups_of,
        tiled=True,
    )
    slices = exchange(partial)
    slices = slices.reshape(n_row, cols // n_row, npan)

    early = list(range(1, groups // 2))
    late = list(range(groups // 2, groups)) + [0]
    shared = (counts, block_present.T, proj_count[None, :], coupling.transpose(1, 0, 2))
    u_early, t_early, mark, to_next, to_last = couple(early, *shared, (), v_hbm, panel, other)
    up = [(i, (i + 1) % n_row) for i in range(n_row)]
    before = lax.ppermute(to_next, "row", up)
    copies = mix(col, mark, slices, factor)
    after = lax.ppermute(to_last, "row", [(j, i) for i, j in up])
    mixing = exchange(copies.reshape(cols, npan))
    u_late, t_late, _ = couple(late, *shared, (before, after), v_hbm, panel, other)

    weights = (occ_mask.astype(F32) * occ_weight / (cols * n_col))[None, :]
    us, ts = [in_hbm(u_early), in_hbm(u_late)], [in_hbm(t_early), in_hbm(t_late)]
    vectors, own_part, other_part = finish(
        (early, late), col, mixing, weights, panel, other, us, ts, v_hbm
    )
    density = own_part + lax.ppermute(other_part, "col", [(0, 1), (1, 0)])
    return vectors, density


def solution(mesh):
    placed = (
        P("row", "col"),
        P("row", "col"),
        P(),
        P("row", None),
        P("row"),
        P("row", None, None),
        P("row", None),
        P("col"),
        P("col"),
    )
    return jax.shard_map(
        local,
        mesh=mesh,
        in_specs=placed,
        out_specs=(P("row", "col"), P(("row", "col"), None)),
        check_vma=False,
    )
```

```python
import functools

import jax
import jax.numpy as jnp
from jax import lax
from jax.experimental import pallas as pl
from jax.experimental.pallas import tpu as pltpu
from jax.sharding import PartitionSpec as P

NPMAX = 16
BMAX = 24
K = 9
RIM = 4
EDGE = RIM * BMAX
TAIL = 128
GROUP = 16
SPAN = GROUP + 2 * RIM
WIDE = 640
ALIGN = 64
MIB = 1024 * 1024

VM = pltpu.MemorySpace.VMEM
SM = pltpu.MemorySpace.SMEM
NT = (((1,), (1,)), ((), ()))
NN = (((1,), (0,)), ((), ()))


def dot(a, b, dims=NN, **kw):
    return lax.dot_general(a, b, dims, preferred_element_type=jnp.float32, **kw)


def iota(shape, dim):
    return lax.broadcasted_iota(jnp.int32, shape, dim)


def padded_rows(counts_ref, first_atom, first_row, sources):
    slot = iota((EDGE, 1), 0)
    target = jnp.full((EDGE, 1), -1, jnp.int32)
    row = first_row
    for t in range(RIM):
        count = counts_ref[first_atom + t]
        u = slot - t * BMAX
        target = jnp.where((u >= 0) & (u < count), row + u, target)
        row = row + count
    pick = (iota((EDGE, TAIL), 1) == target).astype(jnp.float32).astype(jnp.bfloat16)
    return [dot(pick, source).astype(jnp.bfloat16) for source in sources]


def fill_rims(counts_ref, e_ref, p_ref, to_next, to_last):
    atoms = counts_ref.shape[0]
    cols = e_ref.shape[1]
    end = e_ref.shape[0] - EDGE
    tail = counts_ref[atoms - 1]
    for t in range(1, RIM):
        tail = tail + counts_ref[atoms - 1 - t]
    for out, atom, row, at in (
        (to_next, atoms - RIM, TAIL - tail, slice(end - TAIL, end)),
        (to_last, 0, 0, slice(EDGE, EDGE + TAIL)),
    ):
        pieces = padded_rows(counts_ref, atom, row, [e_ref[at, :], p_ref[at, :]])
        out[:, :cols] = pieces[0]
        out[:, cols:] = pieces[1]


def pre_kernel(
    which_groups,
    rim_refs,
    counts_ref,
    present_ref,
    proj_ref,
    cm_ref,
    before_ref,
    after_ref,
    v_hbm,
    own_hbm,
    other_hbm,
    u_hbm,
    t_hbm,
    mark_ref,
    pos_ref,
    cp_ref,
    mask_ref,
    column_ref,
    e_ref,
    p_ref,
    u_ref,
    t_ref,
    sem,
    out_sem,
):
    atoms = counts_ref.shape[0]
    rows, cols = v_hbm.shape
    half = own_hbm.shape[1]
    inner = pl.ds(EDGE, rows)
    copies = [
        pltpu.make_async_copy(v_hbm, e_ref.at[inner], sem.at[0]),
        pltpu.make_async_copy(own_hbm, p_ref.at[inner, pl.ds(0, half)], sem.at[1]),
        pltpu.make_async_copy(other_hbm, p_ref.at[inner, pl.ds(half, half)], sem.at[2]),
    ]
    for c in copies:
        c.start()
    out_copies = []
    for halo_ref, at in ((before_ref, 0), (after_ref, EDGE + rows)):
        mine = slice(at, at + EDGE)
        if halo_ref is None:
            e_ref[mine, :] = jnp.zeros((EDGE, cols), jnp.bfloat16)
            p_ref[mine, :] = jnp.zeros((EDGE, 2 * half), jnp.bfloat16)
        else:
            e_ref[mine, :] = halo_ref[:, :cols]
            p_ref[mine, :] = halo_ref[:, cols:]
    mark_ref[0] = counts_ref[0]

    for t in range(RIM):
        pos_ref[t] = t * BMAX
        pos_ref[RIM + atoms + t] = EDGE + rows + t * BMAX

    def add(t, at):
        pos_ref[RIM + t] = at
        return at + counts_ref[t]

    lax.fori_loop(0, atoms, add, jnp.int32(EDGE), unroll=8)
    mask_ref[...] = jnp.zeros(mask_ref.shape, jnp.float32)
    mask_ref[:K, :] = present_ref[...].astype(jnp.float32)
    mask_ref[K : K + 1, :] = proj_ref[...].astype(jnp.float32)
    column_ref[...] = mask_ref[...].T
    lanes = NPMAX * BMAX
    lane = iota((8, WIDE), 1)
    which = lane // BMAX
    slot = lane - which * BMAX
    sub = iota((GROUP, lanes), 1) // BMAX
    starts, bands = [], []

    def multiply(n):
        if n == 0:
            for c in copies:
                c.wait()
            if rim_refs is not None:
                fill_rims(counts_ref, e_ref, p_ref, *rim_refs)
        window = pl.ds(pl.multiple_of(starts[n], ALIGN), WIDE)
        u_ref[n] = dot(bands[n], e_ref[window, :]).astype(jnp.bfloat16)
        t_ref[n] = dot(bands[n], p_ref[window, :]).astype(jnp.bfloat16)
        out_copies.append(pltpu.make_async_copy(u_ref.at[n], u_hbm.at[n], out_sem.at[0, n]))
        out_copies.append(pltpu.make_async_copy(t_ref.at[n], t_hbm.at[n], out_sem.at[1, n]))
        for c in out_copies[-2:]:
            c.start()

    for n, g in enumerate(which_groups):
        mine = slice(g * GROUP, (g + 1) * GROUP)
        first = pos_ref[g * GROUP]
        start = jnp.minimum((first // ALIGN) * ALIGN, rows + 2 * EDGE - WIDE)
        target = jnp.full((8, WIDE), -1, jnp.int32)
        for t in range(SPAN):
            atom = g * GROUP + t - RIM
            count = counts_ref[atom] if 0 <= atom < atoms else BMAX
            at = pos_ref[atom + RIM] - start
            target = jnp.where((which == t) & (slot < count), at + slot, target)
        pick = (iota((WIDE, WIDE), 0) == target[:1]).astype(jnp.float32).astype(jnp.bfloat16)
        kept = column_ref[mine, K : K + 1] > sub.astype(jnp.float32)
        x = []
        for k in range(K):
            block = cm_ref[k, mine, :].astype(jnp.float32)
            x.append(jnp.where((column_ref[mine, k : k + 1] > 0.0) & kept, block, 0.0))
        x += [None] * (NPMAX - K)
        for bit in (1, 2, 4, 8):
            low = (sub & bit) == 0
            new = list(x)
            for p in range(NPMAX):
                q = p + bit
                if p & bit or (x[p] is None and x[q] is None):
                    continue
                a, b = x[p], x[q]
                zero = jnp.zeros((GROUP, lanes), jnp.float32)
                b_up = zero if b is None else pltpu.roll(b, bit * BMAX, 1)
                a_down = zero if a is None else pltpu.roll(a, lanes - bit * BMAX, 1)
                new[p] = jnp.where(low, zero if a is None else a, b_up)
                new[q] = jnp.where(low, a_down, zero if b is None else b)
            x = new
        pad = jnp.zeros((GROUP, WIDE - lanes), jnp.float32)
        for i in range(NPMAX):
            wide = jnp.concatenate([x[i], pad], axis=1)
            halves = [wide[:8], pltpu.roll(wide[8:], 8 * BMAX, 1)]
            for _ in range(2):
                halves = [pltpu.roll(h, 0, 1, stride=BMAX // 2, stride_axis=0) for h in halves]
            skew = jnp.concatenate(halves, axis=0)
            cp_ref[n, i * GROUP : (i + 1) * GROUP, :] = skew.astype(jnp.bfloat16)
        bands.append(dot(cp_ref[n], pick, NT).astype(jnp.bfloat16))
        starts.append(start)
        multiply(n)
    for c in out_copies:
        c.wait()


def own_kernel(own_hbm, v_hbm, done_ref, v_ref, own_ref, acc_ref, sem):
    rows = v_hbm.shape[0]
    blocks = rows // 256
    at = [pl.ds(b * 256, 256) for b in range(blocks)]
    copies = [pltpu.make_async_copy(own_hbm, own_ref, sem.at[blocks])]
    copies += [pltpu.make_async_copy(v_hbm.at[s], v_ref.at[s], sem.at[b]) for b, s in enumerate(at)]
    for c in copies:
        c.start()
    copies[0].wait()
    turned = own_ref[...].T
    for b in range(blocks):
        copies[1 + b].wait()
        mine = slice(b * 256, (b + 1) * 256)
        product = dot(turned[:, mine], v_ref[mine, :])
        acc_ref[...] = product if b == 0 else acc_ref[...] + product
    done_ref[...] = acc_ref[...].T.astype(jnp.bfloat16)


def other_kernel(done_ref, other_ref, v_ref, out_ref):
    half = other_ref.shape[1]
    cols = v_ref.shape[1]
    turned = other_ref[...].T
    out_ref[:, :half] = done_ref[...]
    for at in range(0, cols, 256):
        mine = slice(at, at + 256)
        out_ref[mine, half:] = dot(turned, v_ref[:, mine]).T.astype(jnp.bfloat16)


def mix_kernel(col_ref, mark_ref, parts_ref, factor_ref, out_ref):
    total = jnp.sum(parts_ref[...].astype(jnp.float32), axis=0)
    half = total.shape[1] // 2
    swap = col_ref[0] == 1
    total = jnp.where(swap, pltpu.roll(total, half, 1), total)
    mixed = dot(total, factor_ref[...], precision=lax.Precision.HIGHEST)
    mixed = jnp.where(swap, pltpu.roll(mixed, half, 1), mixed).astype(jnp.bfloat16)
    out_ref[...] = jnp.broadcast_to(mixed[None], out_ref.shape)


def main_kernel(parts, col_ref, mix_ref, weight_ref, own_ref, other_ref, *refs):
    n_parts = len(parts)
    u_hbms, t_hbms = refs[:n_parts], refs[n_parts : 2 * n_parts]
    v_hbm, vectors_hbm, own_out, other_out = refs[2 * n_parts : 2 * n_parts + 4]
    mt_ref, v_ref, u_ref, t_ref, r_ref, d_ref, v_sem, u_sem, out_sem = refs[2 * n_parts + 4 :]
    rows, cols = v_hbm.shape
    blocks = rows // 256
    order = [(g, p, at) for p, part in enumerate(parts) for at, g in enumerate(part)]
    v_copies, out_copies, u_copies = [], [], []
    for b in range(blocks):
        at = pl.ds(b * 256, 256)
        v_copies.append(pltpu.make_async_copy(v_hbm.at[at], v_ref.at[at], v_sem.at[b]))
        out_copies.append(pltpu.make_async_copy(r_ref.at[at], vectors_hbm.at[at], out_sem.at[b]))
    for n, (_, p, at) in enumerate(order):
        u_copies.append(
            [
                pltpu.make_async_copy(u_hbms[p].at[at], u_ref.at[n], u_sem.at[0, n]),
                pltpu.make_async_copy(t_hbms[p].at[at], t_ref.at[n], u_sem.at[1, n]),
            ]
        )
    early, late = range(len(order) // 2), range(len(order) // 2, len(order))
    for n in early:
        for c in u_copies[n]:
            c.start()
    for c in v_copies:
        c.start()
    for n in late:
        for c in u_copies[n]:
            c.start()
    mt_ref[...] = mix_ref[...].T
    mix = mt_ref[...]
    weight = weight_ref[...]
    down, along = iota((256, 256), 0), iota((256, 256), 1)
    same_atom = (down & (GROUP - 1)) == (along & (GROUP - 1))
    spread = ((down >> 4) == (along & (NPMAX - 1))).astype(jnp.float32).astype(jnp.bfloat16)
    same_i = (down >> 4) == (along >> 4)

    def rotate(b):
        at = slice(b * 256, (b + 1) * 256)
        panel = jnp.concatenate([own_ref[at, :], other_ref[at, :]], axis=1)
        turned = v_ref[at, :].astype(jnp.float32) - dot(panel, mix)
        r_ref[at, :] = turned.astype(jnp.bfloat16)

    def project(n):
        turned = u_ref[n].astype(jnp.float32) - dot(t_ref[n], mix)
        return turned.astype(jnp.bfloat16)

    def pair(rounded):
        weighted = (rounded.astype(jnp.float32) * weight).astype(jnp.bfloat16)
        return jnp.where(same_atom, dot(weighted, rounded, NT), 0.0)

    def pack(n, pairs):
        high = pairs.astype(jnp.bfloat16)
        low = (pairs - high.astype(jnp.float32)).astype(jnp.bfloat16)
        spreaded = jnp.where(same_i, dot(high, spread) + dot(low, spread), 0.0)
        total = spreaded[:GROUP]
        for i in range(1, NPMAX):
            total = total + spreaded[i * GROUP : (i + 1) * GROUP]
        at = order[n][0] * GROUP
        d_ref[at : at + GROUP, :] = total

    def densities(which):
        for n in which:
            for c in u_copies[n]:
                c.wait()
        projected, paired = {}, {}
        for n in range(which[0], which[-1] + 3):
            if n in which:
                projected[n] = project(n)
            if n - 1 in which:
                paired[n - 1] = pair(projected.pop(n - 1))
            if n - 2 in which:
                pack(n - 2, paired.pop(n - 2))

    densities(early)
    for c in v_copies:
        c.wait()
    for b in range(blocks):
        rotate(b)
    for c in out_copies:
        c.start()
    densities(late)
    per = own_out.shape[0]
    mine = pl.multiple_of(col_ref[0] * per, per)
    own_out[...] = d_ref[pl.ds(mine, per), :]
    other_out[...] = d_ref[pl.ds(per - mine, per), :]
    for c in out_copies:
        c.wait()


VMEM_SPEC = pl.BlockSpec(memory_space=VM)
SMEM_SPEC = pl.BlockSpec(memory_space=SM)
HBM_SPEC = pl.BlockSpec(memory_space=pltpu.MemorySpace.HBM)
BF16, F32 = jnp.bfloat16, jnp.float32


def in_hbm(x):
    return pltpu.with_memory_space_constraint(x, pltpu.MemorySpace.HBM)


def call(kernel, out_shape, in_specs, out_specs, flops, nbytes, mib, **kw):
    return pl.pallas_call(
        kernel,
        out_shape=out_shape,
        in_specs=in_specs,
        out_specs=out_specs,
        compiler_params=pltpu.CompilerParams(vmem_limit_bytes=mib * MIB),
        cost_estimate=pl.CostEstimate(flops=flops, bytes_accessed=nbytes, transcendentals=0),
        **kw,
    )


def partial_sums(panel, other, v_hbm):
    rows, cols = v_hbm.shape
    half = panel.shape[1]
    work = 2 * rows * cols * half
    done, v_vmem = call(
        own_kernel,
        [pltpu.VMEM((cols, half), BF16), pltpu.VMEM((rows, cols), BF16)],
        [HBM_SPEC, HBM_SPEC],
        [VMEM_SPEC, VMEM_SPEC],
        work,
        5 << 20,
        24,
        scratch_shapes=[
            pltpu.VMEM((rows, half), BF16),
            pltpu.VMEM((half, cols), F32),
            pltpu.SemaphoreType.DMA((rows // 256 + 1,)),
        ],
    )(in_hbm(panel), v_hbm)
    return call(
        other_kernel,
        pltpu.VMEM((cols, 2 * half), BF16),
        [VMEM_SPEC] * 3,
        VMEM_SPEC,
        work,
        5 << 20,
        24,
    )(done, other, v_vmem)


def couple(which, counts, present, proj_count, blocks, halos, v_hbm, panel, other):
    rows, cols = v_hbm.shape
    npan = 2 * panel.shape[1]
    atoms = counts.shape[0]
    n = len(which)

    first = not halos

    def kernel(counts_ref, present_ref, proj_ref, cm_ref, *rest):
        ends = (None, None) if first else rest[:2]
        rest = rest[len(halos) :]
        rim_refs = rest[6:8] if first else None
        rest = rest[:6] + rest[8:] if first else rest
        pre_kernel(which, rim_refs, counts_ref, present_ref, proj_ref, cm_ref, *ends, *rest)

    return call(
        kernel,
        [
            pltpu.HBM((n, 256, cols), BF16),
            pltpu.HBM((n, 256, npan), BF16),
            jax.ShapeDtypeStruct((1,), jnp.int32),
        ]
        + [jax.ShapeDtypeStruct((EDGE, cols + npan), BF16)] * (2 if first else 0),
        [SMEM_SPEC] + [VMEM_SPEC] * (3 + len(halos)) + [HBM_SPEC] * 3,
        [HBM_SPEC, HBM_SPEC, SMEM_SPEC] + [VMEM_SPEC] * (2 if first else 0),
        n * 2 * 256 * WIDE * (WIDE + cols + npan),
        10 << 20,
        28,
        scratch_shapes=[
            pltpu.SMEM((atoms + 2 * RIM,), jnp.int32),
            pltpu.VMEM((n, 256, WIDE), BF16),
            pltpu.VMEM((16, atoms), F32),
            pltpu.VMEM((atoms, 16), F32),
            pltpu.VMEM((rows + 2 * EDGE, cols), BF16),
            pltpu.VMEM((rows + 2 * EDGE, npan), BF16),
            pltpu.VMEM((n, 256, cols), BF16),
            pltpu.VMEM((n, 256, npan), BF16),
            pltpu.SemaphoreType.DMA((3,)),
            pltpu.SemaphoreType.DMA((2, n)),
        ],
    )(counts, present, proj_count, blocks, *halos, v_hbm, panel, other)


def mix(col, mark, slices, factor):
    return call(
        mix_kernel,
        pltpu.VMEM(slices.shape, BF16),
        [SMEM_SPEC, SMEM_SPEC, VMEM_SPEC, VMEM_SPEC],
        VMEM_SPEC,
        1 << 24,
        1 << 20,
        8,
    )(col, mark, slices, factor)


def finish(parts, col, mixing, weights, panel, other, us, ts, v_hbm):
    rows, cols = v_hbm.shape
    npan = 2 * panel.shape[1]
    groups = sum(len(p) for p in parts)
    atoms = groups * GROUP
    return call(
        functools.partial(main_kernel, parts),
        [
            jax.ShapeDtypeStruct((rows, cols), BF16),
            jax.ShapeDtypeStruct((atoms // 2, 256), F32),
            jax.ShapeDtypeStruct((atoms // 2, 256), F32),
        ],
        [SMEM_SPEC] + [VMEM_SPEC] * 4 + [HBM_SPEC] * (2 * len(parts) + 1),
        [HBM_SPEC, VMEM_SPEC, VMEM_SPEC],
        6 << 30,
        14 << 20,
        28,
        scratch_shapes=[
            pltpu.VMEM((npan, cols), BF16),
            pltpu.VMEM((rows, cols), BF16),
            pltpu.VMEM((groups, 256, cols), BF16),
            pltpu.VMEM((groups, 256, npan), BF16),
            pltpu.VMEM((rows, cols), BF16),
            pltpu.VMEM((atoms, 256), F32),
            pltpu.SemaphoreType.DMA((rows // 256,)),
            pltpu.SemaphoreType.DMA((2, groups)),
            pltpu.SemaphoreType.DMA((rows // 256,)),
        ],
    )(col, mixing, weights, panel, other, *us, *ts, v_hbm)


def local(
    vectors_in, panel, factor, atom_basis, proj_count, coupling, block_present, occ_mask, occ_weight
):
    cols = vectors_in.shape[1]
    npan = 2 * panel.shape[1]
    counts = atom_basis[0]
    groups = counts.shape[0] // GROUP
    n_row = lax.axis_size("row")
    n_col = lax.axis_size("col")
    col = lax.axis_index("col")[None]
    v_hbm = in_hbm(vectors_in)

    other = lax.ppermute(panel, "col", [(0, 1), (1, 0)])
    partial = partial_sums(panel, other, v_hbm)
    slices = lax.all_to_all(partial, "row", 0, 0, tiled=True)
    slices = slices.reshape(n_row, cols // n_row, npan)

    early = list(range(1, groups // 2 - 2))
    late = list(range(groups // 2 - 2, groups)) + [0]
    shared = (counts, block_present.T, proj_count[None, :], coupling.transpose(1, 0, 2))
    u_early, t_early, mark, to_next, to_last = couple(early, *shared, (), v_hbm, panel, other)
    up = [(i, (i + 1) % n_row) for i in range(n_row)]
    before = lax.ppermute(to_next, "row", up)
    copies = mix(col, mark, slices, factor)
    after = lax.ppermute(to_last, "row", [(j, i) for i, j in up])
    mixing = lax.all_to_all(copies.reshape(cols, npan), "row", 0, 0, tiled=True)
    u_late, t_late, _ = couple(late, *shared, (before, after), v_hbm, panel, other)

    weights = (occ_mask.astype(F32) * occ_weight / (cols * n_col))[None, :]
    us, ts = [in_hbm(u_early), in_hbm(u_late)], [in_hbm(t_early), in_hbm(t_late)]
    vectors, own_part, other_part = finish(
        (early, late), col, mixing, weights, panel, other, us, ts, v_hbm
    )
    density = own_part + lax.ppermute(other_part, "col", [(0, 1), (1, 0)])
    return vectors, density


def solution(mesh):
    placed = (
        P("row", "col"),
        P("row", "col"),
        P(),
        P("row", None),
        P("row"),
        P("row", None, None),
        P("row", None),
        P("col"),
        P("col"),
    )
    return jax.shard_map(
        local,
        mesh=mesh,
        in_specs=placed,
        out_specs=(P("row", "col"), P(("row", "col"), None)),
        check_vma=False,
    )
```

```python
import functools

import jax
import jax.numpy as jnp
from jax import lax
from jax.experimental import pallas as pl
from jax.experimental.pallas import tpu as pltpu
from jax.sharding import PartitionSpec as P

NPMAX = 16
BMAX = 24
K = 9
RIM = 4
EDGE = RIM * BMAX
TAIL = 128
GROUP = 16
SPAN = GROUP + 2 * RIM
WIDE = 640
ALIGN = 64
MIB = 1024 * 1024

VM = pltpu.MemorySpace.VMEM
SM = pltpu.MemorySpace.SMEM
NT = (((1,), (1,)), ((), ()))
NN = (((1,), (0,)), ((), ()))


def dot(a, b, dims=NN, **kw):
    return lax.dot_general(a, b, dims, preferred_element_type=jnp.float32, **kw)


def iota(shape, dim):
    return lax.broadcasted_iota(jnp.int32, shape, dim)


def padded_rows(counts_ref, first_atom, first_row, sources):
    slot = iota((EDGE, 1), 0)
    target = jnp.full((EDGE, 1), -1, jnp.int32)
    row = first_row
    for t in range(RIM):
        count = counts_ref[first_atom + t]
        u = slot - t * BMAX
        target = jnp.where((u >= 0) & (u < count), row + u, target)
        row = row + count
    pick = (iota((EDGE, TAIL), 1) == target).astype(jnp.float32).astype(jnp.bfloat16)
    return [dot(pick, source).astype(jnp.bfloat16) for source in sources]


def fill_rims(counts_ref, e_ref, p_ref, to_next, to_last):
    atoms = counts_ref.shape[0]
    cols = e_ref.shape[1]
    end = e_ref.shape[0] - EDGE
    tail = counts_ref[atoms - 1]
    for t in range(1, RIM):
        tail = tail + counts_ref[atoms - 1 - t]
    for out, atom, row, at in (
        (to_next, atoms - RIM, TAIL - tail, slice(end - TAIL, end)),
        (to_last, 0, 0, slice(EDGE, EDGE + TAIL)),
    ):
        pieces = padded_rows(counts_ref, atom, row, [e_ref[at, :], p_ref[at, :]])
        out[:, :cols] = pieces[0]
        out[:, cols:] = pieces[1]


def pre_kernel(
    which_groups,
    rim_refs,
    counts_ref,
    present_ref,
    proj_ref,
    cm_ref,
    before_ref,
    after_ref,
    v_hbm,
    own_hbm,
    other_hbm,
    u_hbm,
    t_hbm,
    mark_ref,
    pos_ref,
    cp_ref,
    mask_ref,
    column_ref,
    e_ref,
    p_ref,
    u_ref,
    t_ref,
    sem,
    out_sem,
):
    atoms = counts_ref.shape[0]
    rows, cols = v_hbm.shape
    half = own_hbm.shape[1]
    inner = pl.ds(EDGE, rows)
    copies = [
        pltpu.make_async_copy(v_hbm, e_ref.at[inner], sem.at[0]),
        pltpu.make_async_copy(own_hbm, p_ref.at[inner, pl.ds(0, half)], sem.at[1]),
        pltpu.make_async_copy(other_hbm, p_ref.at[inner, pl.ds(half, half)], sem.at[2]),
    ]
    for c in copies:
        c.start()
    out_copies = []
    for halo_ref, at in ((before_ref, 0), (after_ref, EDGE + rows)):
        mine = slice(at, at + EDGE)
        if halo_ref is None:
            e_ref[mine, :] = jnp.zeros((EDGE, cols), jnp.bfloat16)
            p_ref[mine, :] = jnp.zeros((EDGE, 2 * half), jnp.bfloat16)
        else:
            e_ref[mine, :] = halo_ref[:, :cols]
            p_ref[mine, :] = halo_ref[:, cols:]
    mark_ref[0] = counts_ref[0]

    for t in range(RIM):
        pos_ref[t] = t * BMAX
        pos_ref[RIM + atoms + t] = EDGE + rows + t * BMAX

    def add(t, at):
        pos_ref[RIM + t] = at
        return at + counts_ref[t]

    lax.fori_loop(0, atoms, add, jnp.int32(EDGE), unroll=8)
    mask_ref[...] = jnp.zeros(mask_ref.shape, jnp.float32)
    mask_ref[:K, :] = present_ref[...].astype(jnp.float32)
    mask_ref[K : K + 1, :] = proj_ref[...].astype(jnp.float32)
    column_ref[...] = mask_ref[...].T
    lanes = NPMAX * BMAX
    lane = iota((8, WIDE), 1)
    which = lane // BMAX
    slot = lane - which * BMAX
    sub = iota((GROUP, lanes), 1) // BMAX
    starts, bands = [], []

    def multiply(n):
        if n == 0:
            for c in copies:
                c.wait()
            if rim_refs is not None:
                fill_rims(counts_ref, e_ref, p_ref, *rim_refs)
        window = pl.ds(pl.multiple_of(starts[n], ALIGN), WIDE)
        u_ref[n] = dot(bands[n], e_ref[window, :]).astype(jnp.bfloat16)
        t_ref[n] = dot(bands[n], p_ref[window, :]).astype(jnp.bfloat16)
        out_copies.append(pltpu.make_async_copy(u_ref.at[n], u_hbm.at[n], out_sem.at[0, n]))
        out_copies.append(pltpu.make_async_copy(t_ref.at[n], t_hbm.at[n], out_sem.at[1, n]))
        for c in out_copies[-2:]:
            c.start()

    for n, g in enumerate(which_groups):
        mine = slice(g * GROUP, (g + 1) * GROUP)
        first = pos_ref[g * GROUP]
        start = jnp.minimum((first // ALIGN) * ALIGN, rows + 2 * EDGE - WIDE)
        target = jnp.full((8, WIDE), -1, jnp.int32)
        for t in range(SPAN):
            atom = g * GROUP + t - RIM
            count = counts_ref[atom] if 0 <= atom < atoms else BMAX
            at = pos_ref[atom + RIM] - start
            target = jnp.where((which == t) & (slot < count), at + slot, target)
        pick = (iota((WIDE, WIDE), 0) == target[:1]).astype(jnp.float32).astype(jnp.bfloat16)
        kept = column_ref[mine, K : K + 1] > sub.astype(jnp.float32)
        x = []
        for k in range(K):
            block = cm_ref[k, mine, :].astype(jnp.float32)
            x.append(jnp.where((column_ref[mine, k : k + 1] > 0.0) & kept, block, 0.0))
        x += [None] * (NPMAX - K)
        for bit in (1, 2, 4, 8):
            low = (sub & bit) == 0
            new = list(x)
            for p in range(NPMAX):
                q = p + bit
                if p & bit or (x[p] is None and x[q] is None):
                    continue
                a, b = x[p], x[q]
                zero = jnp.zeros((GROUP, lanes), jnp.float32)
                b_up = zero if b is None else pltpu.roll(b, bit * BMAX, 1)
                a_down = zero if a is None else pltpu.roll(a, lanes - bit * BMAX, 1)
                new[p] = jnp.where(low, zero if a is None else a, b_up)
                new[q] = jnp.where(low, a_down, zero if b is None else b)
            x = new
        pad = jnp.zeros((GROUP, WIDE - lanes), jnp.float32)
        for i in range(NPMAX):
            wide = jnp.concatenate([x[i], pad], axis=1)
            halves = [wide[:8], pltpu.roll(wide[8:], 8 * BMAX, 1)]
            for _ in range(2):
                halves = [pltpu.roll(h, 0, 1, stride=BMAX // 2, stride_axis=0) for h in halves]
            skew = jnp.concatenate(halves, axis=0)
            cp_ref[n, i * GROUP : (i + 1) * GROUP, :] = skew.astype(jnp.bfloat16)
        bands.append(dot(cp_ref[n], pick, NT).astype(jnp.bfloat16))
        starts.append(start)
        multiply(n)
    for c in out_copies:
        c.wait()


def own_kernel(own_hbm, v_hbm, done_ref, v_ref, own_ref, acc_ref, sem):
    rows = v_hbm.shape[0]
    blocks = rows // 256
    at = [pl.ds(b * 256, 256) for b in range(blocks)]
    copies = [pltpu.make_async_copy(own_hbm, own_ref, sem.at[blocks])]
    copies += [pltpu.make_async_copy(v_hbm.at[s], v_ref.at[s], sem.at[b]) for b, s in enumerate(at)]
    for c in copies:
        c.start()
    copies[0].wait()
    turned = own_ref[...].T
    for b in range(blocks):
        copies[1 + b].wait()
        mine = slice(b * 256, (b + 1) * 256)
        product = dot(turned[:, mine], v_ref[mine, :])
        acc_ref[...] = product if b == 0 else acc_ref[...] + product
    done_ref[...] = acc_ref[...].T.astype(jnp.bfloat16)


def other_kernel(done_ref, other_ref, v_ref, out_ref):
    half = other_ref.shape[1]
    cols = v_ref.shape[1]
    turned = other_ref[...].T
    out_ref[:, :half] = done_ref[...]
    for at in range(0, cols, 256):
        mine = slice(at, at + 256)
        out_ref[mine, half:] = dot(turned, v_ref[:, mine]).T.astype(jnp.bfloat16)


def mix_kernel(col_ref, mark_ref, parts_ref, factor_ref, out_hbm, some_ref, sem):
    total = jnp.sum(parts_ref[...].astype(jnp.float32), axis=0)
    half = total.shape[1] // 2
    swap = col_ref[0] == 1
    total = jnp.where(swap, pltpu.roll(total, half, 1), total)
    mixed = dot(total, factor_ref[...], precision=lax.Precision.HIGHEST)
    mixed = jnp.where(swap, pltpu.roll(mixed, half, 1), mixed).astype(jnp.bfloat16)
    some_ref[...] = jnp.broadcast_to(mixed[None], some_ref.shape)
    some = some_ref.shape[0]
    copies = []
    for n in range(out_hbm.shape[0] // some):
        at = pl.ds(n * some, some)
        copies.append(pltpu.make_async_copy(some_ref, out_hbm.at[at], sem.at[n]))
        copies[-1].start()
    for c in copies:
        c.wait()


def main_kernel(parts, col_ref, mix_ref, weight_ref, own_ref, other_ref, *refs):
    n_parts = len(parts)
    u_hbms, t_hbms = refs[:n_parts], refs[n_parts : 2 * n_parts]
    v_hbm, vectors_hbm, own_out, other_out = refs[2 * n_parts : 2 * n_parts + 4]
    mt_ref, v_ref, u_ref, t_ref, r_ref, d_ref, v_sem, u_sem, out_sem = refs[2 * n_parts + 4 :]
    rows, cols = v_hbm.shape
    blocks = rows // 256
    order = [(g, p, at) for p, part in enumerate(parts) for at, g in enumerate(part)]
    v_copies, out_copies, u_copies = [], [], []
    for b in range(blocks):
        at = pl.ds(b * 256, 256)
        v_copies.append(pltpu.make_async_copy(v_hbm.at[at], v_ref.at[at], v_sem.at[b]))
        out_copies.append(pltpu.make_async_copy(r_ref.at[at], vectors_hbm.at[at], out_sem.at[b]))
    for n, (_, p, at) in enumerate(order):
        u_copies.append(
            [
                pltpu.make_async_copy(u_hbms[p].at[at], u_ref.at[n], u_sem.at[0, n]),
                pltpu.make_async_copy(t_hbms[p].at[at], t_ref.at[n], u_sem.at[1, n]),
            ]
        )
    early, late = range(len(order) // 2), range(len(order) // 2, len(order))
    for n in early:
        for c in u_copies[n]:
            c.start()
    for c in v_copies:
        c.start()
    for n in late:
        for c in u_copies[n]:
            c.start()
    mt_ref[...] = mix_ref[...].T
    mix = mt_ref[...]
    weight = weight_ref[...]
    down, along = iota((256, 256), 0), iota((256, 256), 1)
    same_atom = (down & (GROUP - 1)) == (along & (GROUP - 1))
    spread = ((down >> 4) == (along & (NPMAX - 1))).astype(jnp.float32).astype(jnp.bfloat16)
    same_i = (down >> 4) == (along >> 4)

    def rotate(b):
        at = slice(b * 256, (b + 1) * 256)
        panel = jnp.concatenate([own_ref[at, :], other_ref[at, :]], axis=1)
        turned = v_ref[at, :].astype(jnp.float32) - dot(panel, mix)
        r_ref[at, :] = turned.astype(jnp.bfloat16)

    def project(n):
        turned = u_ref[n].astype(jnp.float32) - dot(t_ref[n], mix)
        return turned.astype(jnp.bfloat16)

    def pair(rounded):
        weighted = (rounded.astype(jnp.float32) * weight).astype(jnp.bfloat16)
        return jnp.where(same_atom, dot(weighted, rounded, NT), 0.0)

    def pack(n, pairs):
        high = pairs.astype(jnp.bfloat16)
        low = (pairs - high.astype(jnp.float32)).astype(jnp.bfloat16)
        spreaded = jnp.where(same_i, dot(high, spread) + dot(low, spread), 0.0)
        total = spreaded[:GROUP]
        for i in range(1, NPMAX):
            total = total + spreaded[i * GROUP : (i + 1) * GROUP]
        at = order[n][0] * GROUP
        d_ref[at : at + GROUP, :] = total

    def densities(which):
        for n in which:
            for c in u_copies[n]:
                c.wait()
        projected, paired = {}, {}
        for n in range(which[0], which[-1] + 3):
            if n in which:
                projected[n] = project(n)
            if n - 1 in which:
                paired[n - 1] = pair(projected.pop(n - 1))
            if n - 2 in which:
                pack(n - 2, paired.pop(n - 2))

    densities(early)
    for c in v_copies:
        c.wait()
    for b in range(blocks):
        rotate(b)
    for c in out_copies:
        c.start()
    densities(late)
    per = own_out.shape[0]
    mine = pl.multiple_of(col_ref[0] * per, per)
    own_out[...] = d_ref[pl.ds(mine, per), :]
    other_out[...] = d_ref[pl.ds(per - mine, per), :]
    for c in out_copies:
        c.wait()


VMEM_SPEC = pl.BlockSpec(memory_space=VM)
SMEM_SPEC = pl.BlockSpec(memory_space=SM)
HBM_SPEC = pl.BlockSpec(memory_space=pltpu.MemorySpace.HBM)
BF16, F32 = jnp.bfloat16, jnp.float32


def in_hbm(x):
    return pltpu.with_memory_space_constraint(x, pltpu.MemorySpace.HBM)


def call(kernel, out_shape, in_specs, out_specs, flops, nbytes, mib, **kw):
    return pl.pallas_call(
        kernel,
        out_shape=out_shape,
        in_specs=in_specs,
        out_specs=out_specs,
        compiler_params=pltpu.CompilerParams(vmem_limit_bytes=mib * MIB),
        cost_estimate=pl.CostEstimate(flops=flops, bytes_accessed=nbytes, transcendentals=0),
        **kw,
    )


def partial_sums(panel, other, v_hbm):
    rows, cols = v_hbm.shape
    half = panel.shape[1]
    work = 2 * rows * cols * half
    done, v_vmem = call(
        own_kernel,
        [pltpu.VMEM((cols, half), BF16), pltpu.VMEM((rows, cols), BF16)],
        [HBM_SPEC, HBM_SPEC],
        [VMEM_SPEC, VMEM_SPEC],
        work,
        5 << 20,
        24,
        scratch_shapes=[
            pltpu.VMEM((rows, half), BF16),
            pltpu.VMEM((half, cols), F32),
            pltpu.SemaphoreType.DMA((rows // 256 + 1,)),
        ],
    )(in_hbm(panel), v_hbm)
    return call(
        other_kernel,
        pltpu.VMEM((cols, 2 * half), BF16),
        [VMEM_SPEC] * 3,
        VMEM_SPEC,
        work,
        5 << 20,
        24,
    )(done, other, v_vmem)


def couple(which, counts, present, proj_count, blocks, halos, v_hbm, panel, other):
    rows, cols = v_hbm.shape
    npan = 2 * panel.shape[1]
    atoms = counts.shape[0]
    n = len(which)

    first = not halos

    def kernel(counts_ref, present_ref, proj_ref, cm_ref, *rest):
        ends = (None, None) if first else rest[:2]
        rest = rest[len(halos) :]
        rim_refs = rest[6:8] if first else None
        rest = rest[:6] + rest[8:] if first else rest
        pre_kernel(which, rim_refs, counts_ref, present_ref, proj_ref, cm_ref, *ends, *rest)

    return call(
        kernel,
        [
            pltpu.HBM((n, 256, cols), BF16),
            pltpu.HBM((n, 256, npan), BF16),
            jax.ShapeDtypeStruct((1,), jnp.int32),
        ]
        + [jax.ShapeDtypeStruct((EDGE, cols + npan), BF16)] * (2 if first else 0),
        [SMEM_SPEC] + [VMEM_SPEC] * (3 + len(halos)) + [HBM_SPEC] * 3,
        [HBM_SPEC, HBM_SPEC, SMEM_SPEC] + [VMEM_SPEC] * (2 if first else 0),
        n * 2 * 256 * WIDE * (WIDE + cols + npan),
        10 << 20,
        28,
        scratch_shapes=[
            pltpu.SMEM((atoms + 2 * RIM,), jnp.int32),
            pltpu.VMEM((n, 256, WIDE), BF16),
            pltpu.VMEM((16, atoms), F32),
            pltpu.VMEM((atoms, 16), F32),
            pltpu.VMEM((rows + 2 * EDGE, cols), BF16),
            pltpu.VMEM((rows + 2 * EDGE, npan), BF16),
            pltpu.VMEM((n, 256, cols), BF16),
            pltpu.VMEM((n, 256, npan), BF16),
            pltpu.SemaphoreType.DMA((3,)),
            pltpu.SemaphoreType.DMA((2, n)),
        ],
    )(counts, present, proj_count, blocks, *halos, v_hbm, panel, other)


def mix(col, mark, slices, factor):
    return call(
        mix_kernel,
        pltpu.HBM(slices.shape, BF16),
        [SMEM_SPEC, SMEM_SPEC, VMEM_SPEC, VMEM_SPEC],
        HBM_SPEC,
        1 << 24,
        1 << 20,
        8,
        scratch_shapes=[
            pltpu.VMEM((8, *slices.shape[1:]), BF16),
            pltpu.SemaphoreType.DMA((slices.shape[0] // 8,)),
        ],
    )(col, mark, slices, factor)


def finish(parts, col, mixing, weights, panel, other, us, ts, v_hbm):
    rows, cols = v_hbm.shape
    npan = 2 * panel.shape[1]
    groups = sum(len(p) for p in parts)
    atoms = groups * GROUP
    return call(
        functools.partial(main_kernel, parts),
        [
            jax.ShapeDtypeStruct((rows, cols), BF16),
            jax.ShapeDtypeStruct((atoms // 2, 256), F32),
            jax.ShapeDtypeStruct((atoms // 2, 256), F32),
        ],
        [SMEM_SPEC] + [VMEM_SPEC] * 4 + [HBM_SPEC] * (2 * len(parts) + 1),
        [HBM_SPEC, VMEM_SPEC, VMEM_SPEC],
        6 << 30,
        14 << 20,
        28,
        scratch_shapes=[
            pltpu.VMEM((npan, cols), BF16),
            pltpu.VMEM((rows, cols), BF16),
            pltpu.VMEM((groups, 256, cols), BF16),
            pltpu.VMEM((groups, 256, npan), BF16),
            pltpu.VMEM((rows, cols), BF16),
            pltpu.VMEM((atoms, 256), F32),
            pltpu.SemaphoreType.DMA((rows // 256,)),
            pltpu.SemaphoreType.DMA((2, groups)),
            pltpu.SemaphoreType.DMA((rows // 256,)),
        ],
    )(col, mixing, weights, panel, other, *us, *ts, v_hbm)


def local(
    vectors_in, panel, factor, atom_basis, proj_count, coupling, block_present, occ_mask, occ_weight
):
    cols = vectors_in.shape[1]
    npan = 2 * panel.shape[1]
    counts = atom_basis[0]
    groups = counts.shape[0] // GROUP
    n_row = lax.axis_size("row")
    n_col = lax.axis_size("col")
    col = lax.axis_index("col")[None]
    v_hbm = in_hbm(vectors_in)

    other = lax.ppermute(panel, "col", [(0, 1), (1, 0)])
    partial = partial_sums(panel, other, v_hbm)
    slices = lax.all_to_all(partial, "row", 0, 0, tiled=True)
    slices = slices.reshape(n_row, cols // n_row, npan)

    early = list(range(1, groups // 2 - 2))
    late = list(range(groups // 2 - 2, groups)) + [0]
    shared = (counts, block_present.T, proj_count[None, :], coupling.transpose(1, 0, 2))
    u_early, t_early, mark, to_next, to_last = couple(early, *shared, (), v_hbm, panel, other)
    up = [(i, (i + 1) % n_row) for i in range(n_row)]
    before = lax.ppermute(to_next, "row", up)
    copies = mix(col, mark, slices, factor)
    after = lax.ppermute(to_last, "row", [(j, i) for i, j in up])
    mixing = lax.all_to_all(copies.reshape(cols, npan), "row", 0, 0, tiled=True)
    u_late, t_late, _ = couple(late, *shared, (before, after), v_hbm, panel, other)

    weights = (occ_mask.astype(F32) * occ_weight / (cols * n_col))[None, :]
    us, ts = [in_hbm(u_early), in_hbm(u_late)], [in_hbm(t_early), in_hbm(t_late)]
    vectors, own_part, other_part = finish(
        (early, late), col, mixing, weights, panel, other, us, ts, v_hbm
    )
    density = own_part + lax.ppermute(other_part, "col", [(0, 1), (1, 0)])
    return vectors, density


def solution(mesh):
    placed = (
        P("row", "col"),
        P("row", "col"),
        P(),
        P("row", None),
        P("row"),
        P("row", None, None),
        P("row", None),
        P("col"),
        P("col"),
    )
    return jax.shard_map(
        local,
        mesh=mesh,
        in_specs=placed,
        out_specs=(P("row", "col"), P(("row", "col"), None)),
        check_vma=False,
    )
```
